32 devices in a mesh: groups: 2 (over y), query: 16 (over z, x, core).
Axes of the slice: x: 2, y: 2, z: 4, core: 2. Of those that a mesh axis runs over, the one named last changes fastest.
Arguments:
- tokens: bfloat16 [32, 8192], P(('groups', 'query')), parts along dimension 0, may hold values from -6 to 6
- target: bfloat16 [32, 8192], P(('groups', 'query')), parts along dimension 0, may hold values from -6 to 6
- gate_weight: bfloat16 [8192, 28672], P(None, 'query'), may hold values from -0.0625 to 0.0625
- up_weight: bfloat16 [8192, 28672], P(None, 'query'), may hold values from -0.0625 to 0.0625
- down_weight: bfloat16 [28672, 8192], P('query'), may hold values from -0.03125 to 0.03125
- proj_in: bfloat16 [28672, 64], P('query'), may hold values from -0.03125 to 0.03125
- proj_out: bfloat16 [8192, 64], replicated, may hold values from -0.0625 to 0.0625
- segment_ids: int32 [32], P('groups'), parts along dimension 0, may hold values from 0 to 3, never falling along the last dimension, each value on 1 to 8 neighbouring positions
- queries: bfloat16 [1024, 4096], P('query'), may hold values from -0.09375 to 0.09375
Outputs:
- scores: float32 [1024, 8], P('query', 'groups'), parts along dimension 1
The draws below stay inside these ranges and needn't reach their ends.
There are 2 independent parts, one for each index of `groups`. The reference program is written for one: setup_inputs(seed, part) draws one part's arguments, and reference() takes and returns one part's arrays. A program takes and returns all parts, laid end to end along the dimension named above; an argument that names none is the same for every part. Nothing has to cross between parts.
Inputs may be any that keep to these rules, and one draw needn't show every extreme that they name: `segment_ids`: ids never fall along the batch; each of the 4 pieces holds 1 to 8 tokens and one holds exactly 8.
All inputs are finite; a program needn't handle non-finite values.
Results may differ from the reference program's by a relative error of at most 0.0049.
Values may be sent and summed in bfloat16 or wider, within the bound.
A program may use at most 192 MiB of HBM per device.

```python
import math
import jax
import jax.numpy as jnp
import numpy as np
from jax import lax

D = 8192
FF = 28672
R = 64
SEQS = 4
TOKENS = 16
NQ = 1024
MOST = 8


def levels(key, extent, pieces, least, high):
    factor_of, own = 1.0, jax.random.fold_in(key, 6)
    for position, blocks in pieces:
        draws = jnp.exp(jax.random.uniform(jax.random.fold_in(own, position), (blocks,), jnp.float32, least / len(pieces), high / len(pieces)))
        factor_of = factor_of * jnp.repeat(draws, extent[position] // blocks).reshape([-1 if axis == position else 1 for axis in range(len(extent))])
    return factor_of


def length_profile(number_of, total, reach, skew):
    loads = [(1 << 20) // math.isqrt(grade ** skew) + 1 for grade in range(2, number_of + 1)]
    surplus, counts = total - reach - (number_of - 1), [1] * (number_of - 1)
    while surplus > 0:
        free = [i for i in range(number_of - 1) if counts[i] < reach]
        whole, left = sum([loads[i] for i in free]), surplus
        for i in free:
            extra = min(reach - counts[i], max(1, left * loads[i] // whole), surplus)
            counts[i] = counts[i] + extra
            surplus = surplus - extra
    return np.array([reach] + counts)


def uneven_parts(own_key, number_of, total, limit, skew):
    if number_of == 2:
        one = jax.random.randint(own_key, (), max(1, total - limit), min(limit, total - 1) + 1)
        return jnp.stack([one, total - one])
    lengths = jnp.asarray(length_profile(number_of, total, limit, skew), jnp.int32)
    pairs = (number_of - 1) // 2
    donor, sink = lengths[1:1 + 2 * pairs:2], lengths[2:2 + 2 * pairs:2]
    room = jnp.minimum(donor - 1, limit - sink)
    moved = jax.random.randint(jax.random.fold_in(own_key, 1), (pairs,), 0, 1 << 20) % (room + 1)
    lengths = lengths.at[1:1 + 2 * pairs:2].set(donor - moved).at[2:2 + 2 * pairs:2].set(sink + moved)
    return lengths[jax.random.permutation(jax.random.fold_in(own_key, 2), number_of)]


def normal_values(own_key, dims, width, limit, pieces=(), kind=jnp.bfloat16):
    factor_of = levels(own_key, dims, pieces, -0.22, 0.18) if pieces else 1.0
    values = jax.random.normal(own_key, dims, jnp.float32) * width * factor_of
    return jnp.minimum(jnp.maximum(values, -limit), limit).astype(kind)


def setup_inputs(seed: int = 0, part: int = 0) -> dict:
    keys = jax.random.split(jax.random.key(seed), 10)
    own_keys = jax.random.split(jax.random.fold_in(keys[9], part), 10)
    return {
        "tokens": normal_values(own_keys[0], (TOKENS, D), 1.0, 6.0, ((0, 16),)),
        "target": normal_values(own_keys[1], (TOKENS, D), 1.0, 6.0, ((0, 16),)),
        "gate_weight": normal_values(keys[2], (D, FF), D ** -0.5, 0.0625, ((1, 16),)),
        "up_weight": normal_values(keys[3], (D, FF), D ** -0.5, 0.0625, ((1, 16),)),
        "down_weight": normal_values(keys[4], (FF, D), FF ** -0.5, 0.03125, ((0, 16),)),
        "proj_in": normal_values(keys[5], (FF, R), FF ** -0.5, 0.03125, ((0, 16),)),
        "proj_out": normal_values(keys[6], (D, R), D ** -0.5, 0.0625),
        "segment_ids": jnp.searchsorted(jnp.cumsum(uneven_parts(own_keys[7], SEQS, TOKENS, MOST, 1)), jnp.arange(TOKENS), side="right").astype(jnp.int32),
        "queries": normal_values(keys[8], (NQ, R * R), (R * R) ** -0.5, 0.09375, ((0, 16),)),
    }


def reference(tokens, target, gate_weight, up_weight, down_weight, proj_in, proj_out, segment_ids, queries):
    gate_pre = jnp.dot(tokens, gate_weight, preferred_element_type=jnp.float32)
    up_pre = jnp.dot(tokens, up_weight, preferred_element_type=jnp.float32)
    hidden = (jax.nn.silu(gate_pre) * up_pre).astype(jnp.bfloat16)
    output = jnp.dot(hidden, down_weight, preferred_element_type=jnp.float32)
    grad = output - target.astype(jnp.float32)
    input_side = jnp.dot(hidden, proj_in, preferred_element_type=jnp.float32)
    output_side = jnp.dot(grad, proj_out.astype(jnp.float32), precision=lax.Precision.HIGHEST)
    seq_index = jnp.arange(SEQS, dtype=jnp.int32)
    onehot = (segment_ids[None, :] == seq_index[:, None]).astype(jnp.float32)
    masked = onehot[:, :, None] * input_side[None, :, :]
    kronecker = jnp.einsum("sti,tj->sij", masked, output_side, precision=lax.Precision.HIGHEST)
    kronecker = kronecker.reshape(SEQS, R * R).astype(jnp.bfloat16)
    return jnp.dot(queries, kronecker.T, preferred_element_type=jnp.float32)
```

```python
import functools

import jax
import jax.numpy as jnp
from jax import lax
from jax.experimental import pallas as pl
from jax.experimental.pallas import tpu as pltpu
from jax.sharding import PartitionSpec as P

SEQS = 4
DEPTH = 1024
SLOTS = 5
DOWN_SLOTS = 4
CHUNKS = 4
FINE = 8
LANES = 128
F32 = jnp.float32
BF16 = jnp.bfloat16
MESH = pl.DeviceIdType.MESH


def split(value):
    high = value.astype(BF16)
    return high, (value - high.astype(F32)).astype(BF16)


def dot(a, b):
    return jnp.dot(a, b, preferred_element_type=F32)


def dot_lanes(a, b):
    return lax.dot_general(a, b, (((1,), (1,)), ((), ())), preferred_element_type=F32)


def pack(value):
    half = value.shape[0] // 2
    return jnp.concatenate([value[:half], value[half:]], axis=1)


def ring_kernel(
    n, tokens, target, gate, up, down, proj_in, proj_out, segment_ids, queries, scores,
    gate_ring, up_ring, down_ring, pin, pout, tok, tgt, qbuf, slab32, slab, gathered, x32, x16,
    expand, spread, gate_acc, up_acc, hidden_ref, block, side_acc, payload_a, payload_b, parts_a, parts_b,
    gate_sem, up_sem, down_sem, load_sem, tok_send, tok_recv, a_send, a_recv, b_send, b_recv,
):
    me = lax.axis_index("query")
    width = gate.shape[0]
    rank = proj_in.shape[0]
    count = x16.shape[0]
    pieces = width // LANES
    steps = width // DEPTH
    slots = gate_ring.shape[0]
    down_slots = down_ring.shape[0]

    def peer(d):
        return lax.rem(me + d, n)

    barrier = pltpu.get_barrier_semaphore()

    @pl.loop(1, n)
    def _(d):
        pl.semaphore_signal(barrier, inc=1, device_id={"query": peer(d)}, device_id_type=MESH)

    loads = [
        pltpu.make_async_copy(src, dst, load_sem.at[i])
        for i, (src, dst) in enumerate(
            [(tokens, tok), (target, tgt), (proj_out, pout), (proj_in, pin), (queries, qbuf)]
        )
    ]

    def chunk(c):
        return pl.ds(pl.multiple_of(c * DEPTH, DEPTH), DEPTH)

    def ring_copies(c, slot):
        return (
            pltpu.make_async_copy(gate.at[chunk(c), :], gate_ring.at[slot], gate_sem.at[slot]),
            pltpu.make_async_copy(up.at[chunk(c), :], up_ring.at[slot], up_sem.at[slot]),
        )

    def down_copy(c):
        slot = lax.rem(c, down_slots)
        return pltpu.make_async_copy(down.at[:, chunk(c)], down_ring.at[slot], down_sem.at[slot])

    for load in loads[:3]:
        load.start()
    for c in range(slots):
        for copy in ring_copies(c, c):
            copy.start()
    loads[3].start()
    loads[4].start()

    loads[0].wait()
    for k in range(pieces):
        slab32[k : k + 1, :] = tok[:, k * LANES : (k + 1) * LANES].astype(F32)
    slab[...] = slab32[...].astype(BF16)
    gathered[me] = slab[...]

    pl.semaphore_wait(barrier, n - 1)

    def push(src, dst, send, recv, d, slot):
        return pltpu.make_async_remote_copy(
            src_ref=src,
            dst_ref=dst.at[slot],
            send_sem=send.at[d],
            recv_sem=recv.at[slot],
            device_id={"query": peer(d)},
            device_id_type=MESH,
        )

    token_push = functools.partial(push, slab, gathered, tok_send, tok_recv)
    a_push = functools.partial(push, payload_a, parts_a, a_send, a_recv)
    b_push = functools.partial(push, payload_b, parts_b, b_send, b_recv)

    def start_all(copy):
        @pl.loop(1, n)
        def _(d):
            copy(d, me).start()

    def receive_all(copy):
        @pl.loop(1, n)
        def _(d):
            copy(d, peer(d)).wait_recv()

    start_all(token_push)

    owner = lax.broadcasted_iota(jnp.int32, expand.shape, 1) // rank
    expand[...] = jnp.where(
        lax.broadcasted_iota(jnp.int32, expand.shape, 0) == owner, 1.0, 0.0
    ).astype(BF16)
    gate_acc[...] = jnp.zeros_like(gate_acc)
    up_acc[...] = jnp.zeros_like(up_acc)
    side_acc[...] = jnp.zeros_like(side_acc)
    loads[1].wait()
    loads[2].wait()
    target_side = dot_lanes(tgt[...], pout[...])

    receive_all(token_push)
    x32[...] = gathered[...].reshape(n * pieces, LANES).astype(F32)
    for k in range(pieces):
        x16[:, k * LANES : (k + 1) * LANES] = x32[pl.ds(k, n, stride=pieces), :].astype(BF16)

    @pl.loop(0, steps)
    def _(c):
        slot = lax.rem(c, slots)
        for copy in ring_copies(c, slot):
            copy.wait()
        x = x16[:, chunk(c)]
        gate_acc[...] += dot(x, gate_ring[slot])
        up_acc[...] += dot(x, up_ring[slot])

        @pl.when(c + slots < steps)
        def _():
            for copy in ring_copies(c + slots, slot):
                copy.start()

        @pl.when(c < down_slots)
        def _():
            down_copy(c).start()

    gate_pre = gate_acc[...]
    hidden = (gate_pre / (1.0 + jnp.exp(-gate_pre)) * up_acc[...]).astype(BF16)
    hidden_ref[...] = hidden
    loads[3].wait()
    payload_a[...] = pack(dot_lanes(hidden, pin[...]))
    start_all(a_push)
    parts_a[me] = payload_a[...]

    def down_dot(c):
        down_copy(c).wait()
        high, low = split(dot(hidden_ref[...], down_ring[lax.rem(c, down_slots)]))
        return jnp.concatenate([high, low], axis=0)

    def project(c):
        side_acc[...] += dot_lanes(block[...], pout[:, chunk(c)])

    def refill(c):
        @pl.when(c + down_slots < steps)
        def _():
            down_copy(c + down_slots).start()

    block[...] = down_dot(0)
    refill(0)

    @pl.loop(1, steps)
    def _(c):
        new = down_dot(c)
        project(c - 1)
        block[...] = new
        refill(c)

    project(steps - 1)

    def sum_parts(parts):
        return lax.fori_loop(
            0, n, lambda p, t: t + parts[p], jnp.zeros(parts.shape[1:], F32), unroll=8
        )

    side = side_acc[:count, :] + side_acc[count:, :]
    own_row = lax.broadcasted_iota(jnp.int32, side.shape, 0) == me
    side = side - jnp.where(own_row, jnp.broadcast_to(target_side, side.shape), 0.0)
    payload_b[...] = pack(side)
    start_all(b_push)
    parts_b[me] = payload_b[...]
    segments = jnp.concatenate([segment_ids[...], segment_ids[...]], axis=1)
    marks = (
        lax.broadcasted_iota(jnp.int32, (2 * SEQS, 2 * count), 0) == segments
    ).astype(BF16)

    receive_all(a_push)
    total = sum_parts(parts_a)
    input_side = jnp.concatenate([total[:, :rank], total[:, rank:]], axis=0)
    high, low = split(input_side)
    wide = dot(jnp.concatenate([high, low], axis=0), expand[...])
    spread[...] = wide[:count] + wide[count:]
    loads[4].wait()

    @pl.loop(1, n)
    def _(d):
        token_push(d, me).wait_send()
        a_push(d, me).wait_send()
        b_push(d, me).wait_send()

    receive_all(b_push)
    total = sum_parts(parts_b)
    first, second = total[:, :rank], total[:, rank:]
    doubled = jnp.concatenate(
        [jnp.concatenate([first, first], axis=1), jnp.concatenate([second, second], axis=1)],
        axis=0,
    )
    pairs = spread[...] * jnp.concatenate([doubled] * (rank // 2), axis=1)
    high, low = split(pairs)
    kronecker = dot(marks, jnp.concatenate([high, low], axis=0))
    scores[...] = dot_lanes(kronecker.astype(BF16), qbuf[...])[:SEQS]


def pair_kernel(
    n, tokens, target, gate, up, down, proj_in, proj_out, segment_ids, queries, scores,
    gate_v, up_v, down_v, pin, pout, tok, tgt, qbuf, slab32, slab, gathered, x32, x16,
    gate_acc, up_acc, side_t, factors, payload, sibling_part, reduced, parts, kron,
    gate_sem, up_sem, down_sem, load_sem, tok_send, tok_recv, fwd_send, fwd_recv,
    pre_send, pre_recv, part_send, part_recv,
):
    g = lax.axis_index("groups")
    me = lax.axis_index("query")
    core = lax.rem(me, 2)
    sibling = me + 1 - 2 * core
    columns = n // 2
    chips = 2 * columns
    chip = g * columns + lax.div(me, 2)
    own = core * chips + chip
    width = gate.shape[0]
    half = gate_v.shape[1]
    rank = proj_in.shape[0]
    chunks = gathered.shape[0]
    rows = gathered.shape[2]
    span = width // chunks
    fine = gate_sem.shape[0]
    step = width // fine
    per = fine // chunks

    barrier = pltpu.get_barrier_semaphore()

    @pl.loop(1, 2 * n)
    def _(d):
        other = lax.rem(g * n + me + d, 2 * n)
        pl.semaphore_signal(
            barrier, inc=1, device_id=(lax.div(other, n), lax.rem(other, n)), device_id_type=MESH
        )

    units = pl.ds(pl.multiple_of(g * half, LANES), half)

    def cut(c):
        return pl.ds(pl.multiple_of(c * step, step), step)

    loads = [
        pltpu.make_async_copy(src, dst, load_sem.at[i])
        for i, (src, dst) in enumerate(
            [
                (tokens, tok), (proj_out, pout), (target, tgt),
                (proj_in.at[:, units], pin), (queries, qbuf),
            ]
        )
    ]

    def down_copy(c):
        return pltpu.make_async_copy(down.at[units, cut(c)], down_v.at[:, cut(c)], down_sem.at[c])

    def gate_copies(c):
        return (
            pltpu.make_async_copy(gate.at[cut(c), units], gate_v.at[cut(c), :], gate_sem.at[c]),
            pltpu.make_async_copy(up.at[cut(c), units], up_v.at[cut(c), :], up_sem.at[c]),
        )

    loads[0].start()
    loads[1].start()

    @pl.loop(0, fine)
    def _(c):
        down_copy(c).start()

    for load in loads[2:4]:
        load.start()

    @pl.loop(0, fine)
    def _(c):
        for copy in gate_copies(c):
            copy.start()

    loads[4].start()

    loads[0].wait()
    for k in range(width // LANES):
        slab32[k : k + 1, :] = tok[:, k * LANES : (k + 1) * LANES].astype(F32)
    slab[...] = slab32[...].astype(BF16)
    for c in range(chunks):
        gathered[c, own] = slab[c * rows : (c + 1) * rows, :]

    pl.semaphore_wait(barrier, 2 * n - 1)

    def token_push(c, d, slot):
        other = lax.rem(chip + d, chips)
        return pltpu.make_async_remote_copy(
            src_ref=slab.at[pl.ds(pl.multiple_of(c * rows, rows), rows), :],
            dst_ref=gathered.at[c, slot],
            send_sem=tok_send.at[c, d],
            recv_sem=tok_recv.at[c, slot],
            device_id=(lax.div(other, columns), 2 * lax.rem(other, columns) + core),
            device_id_type=MESH,
        )

    def forward(c, owner):
        block = gathered.at[c, pl.ds(owner * chips, chips)]
        return pltpu.make_async_remote_copy(
            src_ref=block, dst_ref=block, send_sem=fwd_send.at[c], recv_sem=fwd_recv.at[c],
            device_id=(g, sibling), device_id_type=MESH,
        )

    @pl.loop(0, chunks)
    def _(c):
        @pl.loop(1, chips)
        def _(d):
            token_push(c, d, own).start()

    gate_acc[...] = jnp.zeros_like(gate_acc)
    up_acc[...] = jnp.zeros_like(up_acc)
    side_t[...] = jnp.zeros_like(side_t)
    loads[1].wait()

    @pl.loop(0, fine)
    def _(c):
        down_copy(c).wait()
        side_t[...] += dot_lanes(pout[:, cut(c)], down_v[:, cut(c)])

    loads[2].wait()
    target_side = dot_lanes(tgt[...], pout[...])
    target_row = jnp.concatenate([jnp.zeros_like(target_side), target_side], axis=1)
    high, low = split(side_t[...])
    loads[3].wait()
    for k in range(half // LANES):
        lanes = slice(k * LANES, (k + 1) * LANES)
        x32[k * rank : (k + 1) * rank, :] = pin[:, lanes].astype(F32)
        for parity in range(2):
            factors[parity * (rank // 2) : (parity + 1) * (rank // 2), lanes] = x32[
                pl.ds(k * rank + parity, rank // 2, stride=2), :
            ].astype(BF16)
    factors[rank : 2 * rank, :] = high
    factors[2 * rank : 3 * rank, :] = jnp.zeros_like(high)
    factors[3 * rank : 4 * rank, :] = low

    def relay(c):
        @pl.loop(1, chips)
        def _(d):
            token_push(c, d, core * chips + lax.rem(chip + d, chips)).wait_recv()

        forward(c, core).start()

    relay(0)

    @pl.loop(0, chunks)
    def _(c):
        @pl.when(c + 1 < chunks)
        def _():
            relay(c + 1)

        forward(c, 1 - core).wait_recv()
        x32[0 : 2 * n * rows, :] = gathered[c].reshape(2 * n * rows, LANES).astype(F32)
        for k in range(rows):
            x16[:, k * LANES : (k + 1) * LANES] = x32[pl.ds(k, 2 * n, stride=rows), :].astype(BF16)
        for i in range(per):
            for copy in gate_copies(c * per + i):
                copy.wait()
        here = pl.ds(pl.multiple_of(c * span, span), span)
        gate_acc[...] += dot(x16[...], gate_v[here, :])
        up_acc[...] += dot(x16[...], up_v[here, :])

    gate_pre = gate_acc[...]
    hidden = (gate_pre / (1.0 + jnp.exp(-gate_pre)) * up_acc[...]).astype(BF16)
    sides = dot_lanes(hidden, factors[...])
    sides = sides[:, :LANES] + sides[:, LANES:]
    own_row = lax.broadcasted_iota(jnp.int32, sides.shape, 0) == own
    sides = sides - jnp.where(own_row, jnp.broadcast_to(target_row, sides.shape), 0.0)
    eight = columns
    for k in range(2):
        payload[k, :eight] = sides[k * eight : (k + 1) * eight]
        payload[k, eight:] = sides[chips + k * eight : chips + (k + 1) * eight]

    merge = pltpu.make_async_remote_copy(
        src_ref=payload.at[1 - core], dst_ref=sibling_part, send_sem=pre_send, recv_sem=pre_recv,
        device_id=(g, sibling), device_id_type=MESH,
    )
    merge.start()

    segment_row = lax.broadcasted_iota(jnp.int32, (n, LANES), 0)
    segment_of = jnp.zeros((n, LANES), jnp.int32)
    for t in range(n):
        segment_of = jnp.where(
            segment_row == (t % 2) * columns + t // 2, segment_ids[t], segment_of
        )
    lane = lax.broadcasted_iota(jnp.int32, (n, LANES), 1)
    quarter = lane // (LANES // SEQS)
    member = quarter == segment_of

    merge.wait_recv()
    total = payload[core] + sibling_part[...]
    reduced[...] = total

    def part_push(d, slot):
        return pltpu.make_async_remote_copy(
            src_ref=reduced, dst_ref=parts.at[slot], send_sem=part_send.at[d],
            recv_sem=part_recv.at[slot], device_id=(core, lax.rem(me + d, n)), device_id_type=MESH,
        )

    @pl.loop(1, n)
    def _(d):
        part_push(d, chip).start()

    @pl.when(core != g)
    def _():
        part_push(0, chip).start()

    @pl.when(core == g)
    def _():
        parts[chip] = reduced[...]

    merge.wait_send()

    @pl.loop(0, chunks)
    def _(c):
        @pl.loop(1, chips)
        def _(d):
            token_push(c, d, own).wait_send()

        forward(c, core).wait_send()

    loads[4].wait()

    @pl.loop(1, chips)
    def _(d):
        part_push(0, lax.rem(chip + d, chips)).wait_recv()

    @pl.when(core != g)
    def _():
        part_push(0, chip).wait_recv()

    total = parts[0]
    for p in range(1, chips):
        total = total + parts[p]
    turned = [total] + [pltpu.roll(total, LANES // SEQS * k, axis=1) for k in range(1, SEQS)]

    def tiled(offset):
        out = turned[-offset % SEQS]
        for k in range(1, SEQS):
            out = jnp.where(quarter == k, turned[(k - offset) % SEQS], out)
        return jnp.where(member, out, 0.0)

    left = jnp.concatenate([tiled(0), tiled(1)], axis=0)
    both = jnp.where(lane < rank, turned[2], total)
    right = jnp.concatenate(
        [jnp.where(lane < rank, both, 0.0), jnp.where(lane < rank, 0.0, both)], axis=0
    )
    left_high, left_low = split(left)
    right_high, right_low = split(right)
    kron[...] = lax.dot_general(
        jnp.concatenate([left_high, left_low, left_high], axis=0),
        jnp.concatenate([right_high, right_high, right_low], axis=0),
        (((0,), (0,)), ((), ())),
        preferred_element_type=F32,
    )
    quarters = LANES // SEQS
    kronecker = jnp.concatenate(
        [kron[pl.ds(k, SEQS, stride=quarters), :] for k in range(quarters)], axis=1
    ).astype(BF16)
    scores[...] = dot_lanes(kronecker, qbuf[...])

    @pl.loop(1, n)
    def _(d):
        part_push(d, chip).wait_send()

    @pl.when(core != g)
    def _():
        part_push(0, chip).wait_send()


def ring_call(n, tokens, target, gate, up, down, proj_in, proj_out, segment_ids, queries):
    width, units = gate.shape
    rank = proj_in.shape[1]
    count = segment_ids.shape[0]
    pieces = width // LANES
    any_spec = pl.BlockSpec(memory_space=pl.ANY)
    vmem_spec = pl.BlockSpec(memory_space=pltpu.VMEM)
    dma = pltpu.SemaphoreType.DMA
    return pl.pallas_call(
        functools.partial(ring_kernel, n),
        out_shape=jax.ShapeDtypeStruct((SEQS, queries.shape[0]), F32),
        in_specs=[any_spec] * 7 + [vmem_spec, any_spec],
        out_specs=vmem_spec,
        scratch_shapes=[
            pltpu.VMEM((SLOTS, DEPTH, units), BF16),
            pltpu.VMEM((SLOTS, DEPTH, units), BF16),
            pltpu.VMEM((DOWN_SLOTS, units, DEPTH), BF16),
            pltpu.VMEM((rank, units), BF16),
            pltpu.VMEM((rank, width), BF16),
            pltpu.VMEM((1, width), BF16),
            pltpu.VMEM((1, width), BF16),
            pltpu.VMEM(queries.shape, BF16),
            pltpu.VMEM((pieces, LANES), F32),
            pltpu.VMEM((pieces, LANES), BF16),
            pltpu.VMEM((n, pieces, LANES), BF16),
            pltpu.VMEM((n * pieces, LANES), F32),
            pltpu.VMEM((count, width), BF16),
            pltpu.VMEM((rank, rank * rank), BF16),
            pltpu.VMEM((count, rank * rank), F32),
            pltpu.VMEM((count, units), F32),
            pltpu.VMEM((count, units), F32),
            pltpu.VMEM((count, units), BF16),
            pltpu.VMEM((2 * count, DEPTH), BF16),
            pltpu.VMEM((2 * count, rank), F32),
            pltpu.VMEM((count // 2, 2 * rank), F32),
            pltpu.VMEM((count // 2, 2 * rank), F32),
            pltpu.VMEM((n, count // 2, 2 * rank), F32),
            pltpu.VMEM((n, count // 2, 2 * rank), F32),
            dma((SLOTS,)),
            dma((SLOTS,)),
            dma((DOWN_SLOTS,)),
            dma((5,)),
            dma((n,)),
            dma((n,)),
            dma((n,)),
            dma((n,)),
            dma((n,)),
            dma((n,)),
        ],
        compiler_params=pltpu.CompilerParams(
            collective_id=1, has_side_effects=True, vmem_limit_bytes=63 * 1024 * 1024
        ),
        name="forget_ring",
    )(
        tokens, target, gate, up, down, proj_in.T, proj_out.T,
        segment_ids.reshape(1, count), queries,
    ).T


def pair_call(n, tokens, target, gate, up, down, proj_in, proj_out, segment_ids, queries):
    width, units = gate.shape
    half = units // 2
    rank = proj_in.shape[1]
    pieces = width // LANES
    rows = pieces // CHUNKS
    any_spec = pl.BlockSpec(memory_space=pl.ANY)
    vmem_spec = pl.BlockSpec(memory_space=pltpu.VMEM)
    smem_spec = pl.BlockSpec(memory_space=pltpu.SMEM)
    dma = pltpu.SemaphoreType.DMA
    return pl.pallas_call(
        functools.partial(pair_kernel, n),
        out_shape=jax.ShapeDtypeStruct((SEQS, queries.shape[0]), F32),
        in_specs=[any_spec] * 7 + [smem_spec, any_spec],
        out_specs=vmem_spec,
        scratch_shapes=[
            pltpu.VMEM((width, half), BF16),
            pltpu.VMEM((width, half), BF16),
            pltpu.VMEM((half, width), BF16),
            pltpu.VMEM((rank, half), BF16),
            pltpu.VMEM((rank, width), BF16),
            pltpu.VMEM((1, width), BF16),
            pltpu.VMEM((1, width), BF16),
            pltpu.VMEM(queries.shape, BF16),
            pltpu.VMEM((pieces, LANES), F32),
            pltpu.VMEM((pieces, LANES), BF16),
            pltpu.VMEM((CHUNKS, 2 * n, rows, LANES), BF16),
            pltpu.VMEM((max(2 * n * rows, half // LANES * rank), LANES), F32),
            pltpu.VMEM((2 * n, width // CHUNKS), BF16),
            pltpu.VMEM((2 * n, half), F32),
            pltpu.VMEM((2 * n, half), F32),
            pltpu.VMEM((rank, half), F32),
            pltpu.VMEM((4 * rank, half), BF16),
            pltpu.VMEM((2, n, LANES), F32),
            pltpu.VMEM((n, LANES), F32),
            pltpu.VMEM((n, LANES), F32),
            pltpu.VMEM((n, n, LANES), F32),
            pltpu.VMEM((LANES, LANES), F32),
            dma((FINE,)),
            dma((FINE,)),
            dma((FINE,)),
            dma((5,)),
            dma((CHUNKS, n)),
            dma((CHUNKS, 2 * n)),
            dma((CHUNKS,)),
            dma((CHUNKS,)),
            dma,
            dma,
            dma((n,)),
            dma((n,)),
        ],
        compiler_params=pltpu.CompilerParams(
            collective_id=0, has_side_effects=True, vmem_limit_bytes=63 * 1024 * 1024
        ),
        name="forget_pair",
    )(tokens, target, gate, up, down, proj_in.T, proj_out.T, segment_ids, queries).T


def solution(mesh):
    n = mesh.shape["query"]
    groups = mesh.shape["groups"]

    def local(tokens, target, gate, up, down, proj_in, proj_out, segment_ids, queries):
        width, units = gate.shape
        shared = (
            groups == 2
            and n == 16
            and segment_ids.shape[0] == n
            and tokens.shape[0] == 1
            and units % (2 * LANES) == 0
            and width % (FINE * LANES) == 0
            and 2 * proj_in.shape[1] == LANES
        )
        call = pair_call if shared else ring_call
        return call(n, tokens, target, gate, up, down, proj_in, proj_out, segment_ids, queries)

    in_specs = (
        P(("groups", "query"), None),
        P(("groups", "query"), None),
        P(None, "query"),
        P(None, "query"),
        P("query", None),
        P("query", None),
        P(),
        P("groups"),
        P("query", None),
    )
    return jax.shard_map(
        local, mesh=mesh, in_specs=in_specs, out_specs=P("query", "groups"), check_vma=False
    )
```

```python
import functools

import jax
import jax.numpy as jnp
from jax import lax
from jax.experimental import pallas as pl
from jax.experimental.pallas import tpu as pltpu
from jax.sharding import PartitionSpec as P

SEQS = 4
DEPTH = 1024
SLOTS = 5
DOWN_SLOTS = 4
CHUNKS = 4
FINE = 8
EARLY = 2
ROWS = 16
LANES = 128
F32 = jnp.float32
BF16 = jnp.bfloat16
MESH = pl.DeviceIdType.MESH


def split(value):
    high = value.astype(BF16)
    return high, (value - high.astype(F32)).astype(BF16)


def dot(a, b):
    return jnp.dot(a, b, preferred_element_type=F32)


def dot_lanes(a, b):
    return lax.dot_general(a, b, (((1,), (1,)), ((), ())), preferred_element_type=F32)


def pack(value):
    half = value.shape[0] // 2
    return jnp.concatenate([value[:half], value[half:]], axis=1)


def ring_kernel(
    n, tokens, target, gate, up, down, proj_in, proj_out, segment_ids, queries, scores,
    gate_ring, up_ring, down_ring, pin, pout, tok, tgt, qbuf, slab32, slab, gathered, x32, x16,
    expand, spread, gate_acc, up_acc, hidden_ref, block, side_acc, payload_a, payload_b, parts_a, parts_b,
    gate_sem, up_sem, down_sem, load_sem, tok_send, tok_recv, a_send, a_recv, b_send, b_recv,
):
    me = lax.axis_index("query")
    width = gate.shape[0]
    rank = proj_in.shape[0]
    count = x16.shape[0]
    pieces = width // LANES
    steps = width // DEPTH
    slots = gate_ring.shape[0]
    down_slots = down_ring.shape[0]

    def peer(d):
        return lax.rem(me + d, n)

    barrier = pltpu.get_barrier_semaphore()

    @pl.loop(1, n)
    def _(d):
        pl.semaphore_signal(barrier, inc=1, device_id={"query": peer(d)}, device_id_type=MESH)

    loads = [
        pltpu.make_async_copy(src, dst, load_sem.at[i])
        for i, (src, dst) in enumerate(
            [(tokens, tok), (target, tgt), (proj_out, pout), (proj_in, pin), (queries, qbuf)]
        )
    ]

    def chunk(c):
        return pl.ds(pl.multiple_of(c * DEPTH, DEPTH), DEPTH)

    def ring_copies(c, slot):
        return (
            pltpu.make_async_copy(gate.at[chunk(c), :], gate_ring.at[slot], gate_sem.at[slot]),
            pltpu.make_async_copy(up.at[chunk(c), :], up_ring.at[slot], up_sem.at[slot]),
        )

    def down_copy(c):
        slot = lax.rem(c, down_slots)
        return pltpu.make_async_copy(down.at[:, chunk(c)], down_ring.at[slot], down_sem.at[slot])

    for load in loads[:3]:
        load.start()
    for c in range(slots):
        for copy in ring_copies(c, c):
            copy.start()
    loads[3].start()
    loads[4].start()

    loads[0].wait()
    for k in range(pieces):
        slab32[k : k + 1, :] = tok[:, k * LANES : (k + 1) * LANES].astype(F32)
    slab[...] = slab32[...].astype(BF16)
    gathered[me] = slab[...]

    pl.semaphore_wait(barrier, n - 1)

    def push(src, dst, send, recv, d, slot):
        return pltpu.make_async_remote_copy(
            src_ref=src,
            dst_ref=dst.at[slot],
            send_sem=send.at[d],
            recv_sem=recv.at[slot],
            device_id={"query": peer(d)},
            device_id_type=MESH,
        )

    token_push = functools.partial(push, slab, gathered, tok_send, tok_recv)
    a_push = functools.partial(push, payload_a, parts_a, a_send, a_recv)
    b_push = functools.partial(push, payload_b, parts_b, b_send, b_recv)

    def start_all(copy):
        @pl.loop(1, n)
        def _(d):
            copy(d, me).start()

    def receive_all(copy):
        @pl.loop(1, n)
        def _(d):
            copy(d, peer(d)).wait_recv()

    start_all(token_push)

    owner = lax.broadcasted_iota(jnp.int32, expand.shape, 1) // rank
    expand[...] = jnp.where(
        lax.broadcasted_iota(jnp.int32, expand.shape, 0) == owner, 1.0, 0.0
    ).astype(BF16)
    gate_acc[...] = jnp.zeros_like(gate_acc)
    up_acc[...] = jnp.zeros_like(up_acc)
    side_acc[...] = jnp.zeros_like(side_acc)
    loads[1].wait()
    loads[2].wait()
    target_side = dot_lanes(tgt[...], pout[...])

    receive_all(token_push)
    x32[...] = gathered[...].reshape(n * pieces, LANES).astype(F32)
    for k in range(pieces):
        x16[:, k * LANES : (k + 1) * LANES] = x32[pl.ds(k, n, stride=pieces), :].astype(BF16)

    @pl.loop(0, steps)
    def _(c):
        slot = lax.rem(c, slots)
        for copy in ring_copies(c, slot):
            copy.wait()
        x = x16[:, chunk(c)]
        gate_acc[...] += dot(x, gate_ring[slot])
        up_acc[...] += dot(x, up_ring[slot])

        @pl.when(c + slots < steps)
        def _():
            for copy in ring_copies(c + slots, slot):
                copy.start()

        @pl.when(c < down_slots)
        def _():
            down_copy(c).start()

    gate_pre = gate_acc[...]
    hidden = (gate_pre / (1.0 + jnp.exp(-gate_pre)) * up_acc[...]).astype(BF16)
    hidden_ref[...] = hidden
    loads[3].wait()
    payload_a[...] = pack(dot_lanes(hidden, pin[...]))
    start_all(a_push)
    parts_a[me] = payload_a[...]

    def down_dot(c):
        down_copy(c).wait()
        high, low = split(dot(hidden_ref[...], down_ring[lax.rem(c, down_slots)]))
        return jnp.concatenate([high, low], axis=0)

    def project(c):
        side_acc[...] += dot_lanes(block[...], pout[:, chunk(c)])

    def refill(c):
        @pl.when(c + down_slots < steps)
        def _():
            down_copy(c + down_slots).start()

    block[...] = down_dot(0)
    refill(0)

    @pl.loop(1, steps)
    def _(c):
        new = down_dot(c)
        project(c - 1)
        block[...] = new
        refill(c)

    project(steps - 1)

    def sum_parts(parts):
        return lax.fori_loop(
            0, n, lambda p, t: t + parts[p], jnp.zeros(parts.shape[1:], F32), unroll=8
        )

    side = side_acc[:count, :] + side_acc[count:, :]
    own_row = lax.broadcasted_iota(jnp.int32, side.shape, 0) == me
    side = side - jnp.where(own_row, jnp.broadcast_to(target_side, side.shape), 0.0)
    payload_b[...] = pack(side)
    start_all(b_push)
    parts_b[me] = payload_b[...]
    segments = jnp.concatenate([segment_ids[...], segment_ids[...]], axis=1)
    marks = (
        lax.broadcasted_iota(jnp.int32, (2 * SEQS, 2 * count), 0) == segments
    ).astype(BF16)

    receive_all(a_push)
    total = sum_parts(parts_a)
    input_side = jnp.concatenate([total[:, :rank], total[:, rank:]], axis=0)
    high, low = split(input_side)
    wide = dot(jnp.concatenate([high, low], axis=0), expand[...])
    spread[...] = wide[:count] + wide[count:]
    loads[4].wait()

    @pl.loop(1, n)
    def _(d):
        token_push(d, me).wait_send()
        a_push(d, me).wait_send()
        b_push(d, me).wait_send()

    receive_all(b_push)
    total = sum_parts(parts_b)
    first, second = total[:, :rank], total[:, rank:]
    doubled = jnp.concatenate(
        [jnp.concatenate([first, first], axis=1), jnp.concatenate([second, second], axis=1)],
        axis=0,
    )
    pairs = spread[...] * jnp.concatenate([doubled] * (rank // 2), axis=1)
    high, low = split(pairs)
    kronecker = dot(marks, jnp.concatenate([high, low], axis=0))
    scores[...] = dot_lanes(kronecker.astype(BF16), qbuf[...])[:SEQS]


def pair_kernel(
    n, tokens, target, gate, up, down, proj_in, proj_out, segment_ids, queries, scores,
    both_v, down_v, pin, pout, tok, tgt, qbuf, slab32, slab, gathered, x32, x16, ids,
    both_acc, side_t, factors, payload, sibling_part, reduced, parts, kron,
    gate_sem, up_sem, down_sem, load_sem, tok_send, tok_recv, fwd_send, fwd_recv,
    pre_send, pre_recv, part_send, part_recv,
):
    g = lax.axis_index("groups")
    me = lax.axis_index("query")
    core = lax.rem(me, 2)
    sibling = me + 1 - 2 * core
    columns = n // 2
    chips = 2 * columns
    chip = g * columns + lax.div(me, 2)
    own = core * chips + chip
    width = gate.shape[0]
    half = both_v.shape[1] // 2
    rank = proj_in.shape[0]
    chunks = gathered.shape[0]
    rows = gathered.shape[2]
    span = width // chunks
    fine = gate_sem.shape[0]
    step = width // fine
    per = fine // chunks

    barrier = pltpu.get_barrier_semaphore()

    def peer(d):
        other = lax.rem(chip + d, chips)
        return lax.div(other, columns), 2 * lax.rem(other, columns) + core

    order = sorted(range(1, chips), key=lambda d: abs(d % columns - columns // 2))
    for d in order:
        pl.semaphore_signal(barrier, inc=1, device_id=peer(d), device_id_type=MESH)
    pl.semaphore_signal(barrier, inc=1, device_id=(g, sibling), device_id_type=MESH)

    units = pl.ds(pl.multiple_of(g * half, LANES), half)

    def cut(c):
        return pl.ds(pl.multiple_of(c * step, step), step)

    loads = [
        pltpu.make_async_copy(src, dst, load_sem.at[i])
        for i, (src, dst) in enumerate(
            [
                (tokens, tok), (proj_out, pout), (target, tgt),
                (proj_in.at[:, units], pin), (queries, qbuf), (segment_ids, ids),
            ]
        )
    ]

    def down_copy(c):
        return pltpu.make_async_copy(down.at[units, cut(c)], down_v.at[:half, cut(c)], down_sem.at[c])

    def gate_copies(c):
        return (
            pltpu.make_async_copy(gate.at[cut(c), units], both_v.at[cut(c), :half], gate_sem.at[c]),
            pltpu.make_async_copy(up.at[cut(c), units], both_v.at[cut(c), half:], up_sem.at[c]),
        )

    for load in loads[:4]:
        load.start()

    @pl.loop(0, fine)
    def _(c):
        down_copy(c).start()

    @pl.loop(0, fine)
    def _(c):
        for copy in gate_copies(c):
            copy.start()

    for load in loads[4:]:
        load.start()

    loads[0].wait()
    for k in range(width // LANES):
        slab32[k : k + 1, :] = tok[:, k * LANES : (k + 1) * LANES].astype(F32)
    slab[...] = slab32[...].astype(BF16)
    for c in range(chunks):
        gathered[c, own] = slab[c * rows : (c + 1) * rows, :]

    def token_push(c, d, slot):
        return pltpu.make_async_remote_copy(
            src_ref=slab.at[pl.ds(pl.multiple_of(c * rows, rows), rows), :],
            dst_ref=gathered.at[c, slot],
            send_sem=tok_send.at[c],
            recv_sem=tok_recv.at[c],
            device_id=peer(d),
            device_id_type=MESH,
        )

    def forward(c, owner):
        block = gathered.at[c, pl.ds(owner * chips, chips)]
        return pltpu.make_async_remote_copy(
            src_ref=block, dst_ref=block, send_sem=fwd_send.at[c], recv_sem=fwd_recv.at[c],
            device_id=(g, sibling), device_id_type=MESH,
        )

    both_acc[...] = jnp.zeros_like(both_acc)
    side_t[...] = jnp.zeros_like(side_t)
    loads[2].wait()
    top = lax.broadcasted_iota(jnp.int32, (ROWS, width), 0) == 0
    down_v[half:, :] = jnp.where(
        top, jnp.broadcast_to(tgt[...].astype(F32), top.shape), 0.0
    ).astype(BF16)
    loads[1].wait()

    def project(c):
        down_copy(c).wait()
        side_t[...] += dot_lanes(pout[:, cut(c)], down_v[:, cut(c)])

    pl.loop(0, EARLY)(project)
    pl.semaphore_wait(barrier, chips)

    @pl.loop(0, chunks)
    def _(c):
        for d in order:
            token_push(c, d, own).start()

        project(c + EARLY)

    pl.loop(EARLY + chunks, fine)(project)
    high, low = split(side_t[...])
    factors[0:rank, half:] = jnp.zeros((rank, ROWS), BF16)
    factors[rank : 2 * rank, :] = high
    factors[2 * rank : 3 * rank, :] = jnp.zeros_like(high)
    factors[3 * rank : 4 * rank, :] = low
    loads[3].wait()
    for k in range(half // LANES):
        lanes = slice(k * LANES, (k + 1) * LANES)
        x32[k * rank : (k + 1) * rank, :] = pin[:, lanes].astype(F32)
        for parity in range(2):
            factors[parity * (rank // 2) : (parity + 1) * (rank // 2), lanes] = x32[
                pl.ds(k * rank + parity, rank // 2, stride=2), :
            ].astype(BF16)

    def all_chips(c, semaphore):
        others = gathered.at[c, pl.ds(0, chips - 1)]
        return pltpu.make_async_copy(others, others, semaphore.at[c])

    def relay(c):
        all_chips(c, tok_recv).wait()
        forward(c, core).start()

    def convert(first, last):
        for k in range(first, last):
            x16[:, k * LANES : (k + 1) * LANES] = x32[pl.ds(k, 2 * n, stride=rows), :].astype(BF16)

    def multiply(c, i):
        here = pl.ds(pl.multiple_of((c * per + i) * step, step), step)
        both_acc[...] += dot(x16[:, i * step : (i + 1) * step], both_v[here, :])

    relay(0)

    @pl.loop(0, chunks)
    def _(c):
        for i in range(per):
            for copy in gate_copies(c * per + i):
                copy.wait()
        forward(c, 1 - core).wait_recv()
        x32[0 : 2 * n * rows, :] = gathered[c].reshape(2 * n * rows, LANES).astype(F32)
        each = rows // per
        convert(0, each)
        for i in range(per - 1):
            multiply(c, i)
            convert((i + 1) * each, (i + 2) * each)

        @pl.when(c + 1 < chunks)
        def _():
            relay(c + 1)

        multiply(c, per - 1)

    gate_pre = both_acc[:, :half]
    hidden = (gate_pre / (1.0 + jnp.exp(-gate_pre)) * both_acc[:, half:]).astype(BF16)
    shape = (2 * n, ROWS)
    own_target = (lax.broadcasted_iota(jnp.int32, shape, 0) == own) & (
        lax.broadcasted_iota(jnp.int32, shape, 1) == 0
    )
    sides = dot_lanes(
        jnp.concatenate([hidden, jnp.where(own_target, -1.0, 0.0).astype(BF16)], axis=1), factors[...]
    )
    sides = sides[:, :LANES] + sides[:, LANES:]
    eight = columns
    for k in range(2):
        payload[k, :eight] = sides[k * eight : (k + 1) * eight]
        payload[k, eight:] = sides[chips + k * eight : chips + (k + 1) * eight]

    merge = pltpu.make_async_remote_copy(
        src_ref=payload.at[1 - core], dst_ref=sibling_part, send_sem=pre_send, recv_sem=pre_recv,
        device_id=(g, sibling), device_id_type=MESH,
    )
    merge.start()

    loads[5].wait()
    segment_row = lax.broadcasted_iota(jnp.int32, (n, LANES), 0)
    segment_of = jnp.zeros((n, LANES), jnp.int32)
    for t in range(n):
        segment_of = jnp.where(
            segment_row == (t % 2) * columns + t // 2, ids[t], segment_of
        )
    lane = lax.broadcasted_iota(jnp.int32, (n, LANES), 1)
    quarter = lane // (LANES // SEQS)
    member = quarter == segment_of

    merge.wait_recv()
    total = payload[core] + sibling_part[...]
    reduced[...] = total

    def part_push(d, slot):
        return pltpu.make_async_remote_copy(
            src_ref=reduced, dst_ref=parts.at[slot], send_sem=part_send.at[d],
            recv_sem=part_recv.at[slot], device_id=(core, lax.rem(me + d, n)), device_id_type=MESH,
        )

    @pl.loop(1, n)
    def _(d):
        part_push(d, chip).start()

    @pl.when(core != g)
    def _():
        part_push(0, chip).start()

    @pl.when(core == g)
    def _():
        parts[chip] = reduced[...]

    merge.wait_send()

    @pl.loop(0, chunks)
    def _(c):
        all_chips(c, tok_send).wait()
        forward(c, core).wait_send()

    loads[4].wait()

    @pl.loop(1, chips)
    def _(d):
        part_push(0, lax.rem(chip + d, chips)).wait_recv()

    @pl.when(core != g)
    def _():
        part_push(0, chip).wait_recv()

    total = parts[0]
    for p in range(1, chips):
        total = total + parts[p]
    turned = [total] + [pltpu.roll(total, LANES // SEQS * k, axis=1) for k in range(1, SEQS)]

    def tiled(offset):
        out = turned[-offset % SEQS]
        for k in range(1, SEQS):
            out = jnp.where(quarter == k, turned[(k - offset) % SEQS], out)
        return jnp.where(member, out, 0.0)

    left = jnp.concatenate([tiled(0), tiled(1)], axis=0)
    both = jnp.where(lane < rank, turned[2], total)
    right = jnp.concatenate(
        [jnp.where(lane < rank, both, 0.0), jnp.where(lane < rank, 0.0, both)], axis=0
    )
    left_high, left_low = split(left)
    right_high, right_low = split(right)
    kron[...] = lax.dot_general(
        jnp.concatenate([left_high, left_low, left_high], axis=0),
        jnp.concatenate([right_high, right_high, right_low], axis=0),
        (((0,), (0,)), ((), ())),
        preferred_element_type=F32,
    )
    quarters = LANES // SEQS
    kronecker = jnp.concatenate(
        [kron[pl.ds(k, SEQS, stride=quarters), :] for k in range(quarters)], axis=1
    ).astype(BF16)
    scores[...] = dot_lanes(kronecker, qbuf[...])

    @pl.loop(1, n)
    def _(d):
        part_push(d, chip).wait_send()

    @pl.when(core != g)
    def _():
        part_push(0, chip).wait_send()


def ring_call(n, tokens, target, gate, up, down, proj_in, proj_out, segment_ids, queries):
    width, units = gate.shape
    rank = proj_in.shape[1]
    count = segment_ids.shape[0]
    pieces = width // LANES
    any_spec = pl.BlockSpec(memory_space=pl.ANY)
    vmem_spec = pl.BlockSpec(memory_space=pltpu.VMEM)
    dma = pltpu.SemaphoreType.DMA
    return pl.pallas_call(
        functools.partial(ring_kernel, n),
        out_shape=jax.ShapeDtypeStruct((SEQS, queries.shape[0]), F32),
        in_specs=[any_spec] * 7 + [vmem_spec, any_spec],
        out_specs=vmem_spec,
        scratch_shapes=[
            pltpu.VMEM((SLOTS, DEPTH, units), BF16),
            pltpu.VMEM((SLOTS, DEPTH, units), BF16),
            pltpu.VMEM((DOWN_SLOTS, units, DEPTH), BF16),
            pltpu.VMEM((rank, units), BF16),
            pltpu.VMEM((rank, width), BF16),
            pltpu.VMEM((1, width), BF16),
            pltpu.VMEM((1, width), BF16),
            pltpu.VMEM(queries.shape, BF16),
            pltpu.VMEM((pieces, LANES), F32),
            pltpu.VMEM((pieces, LANES), BF16),
            pltpu.VMEM((n, pieces, LANES), BF16),
            pltpu.VMEM((n * pieces, LANES), F32),
            pltpu.VMEM((count, width), BF16),
            pltpu.VMEM((rank, rank * rank), BF16),
            pltpu.VMEM((count, rank * rank), F32),
            pltpu.VMEM((count, units), F32),
            pltpu.VMEM((count, units), F32),
            pltpu.VMEM((count, units), BF16),
            pltpu.VMEM((2 * count, DEPTH), BF16),
            pltpu.VMEM((2 * count, rank), F32),
            pltpu.VMEM((count // 2, 2 * rank), F32),
            pltpu.VMEM((count // 2, 2 * rank), F32),
            pltpu.VMEM((n, count // 2, 2 * rank), F32),
            pltpu.VMEM((n, count // 2, 2 * rank), F32),
            dma((SLOTS,)),
            dma((SLOTS,)),
            dma((DOWN_SLOTS,)),
            dma((5,)),
            dma((n,)),
            dma((n,)),
            dma((n,)),
            dma((n,)),
            dma((n,)),
            dma((n,)),
        ],
        compiler_params=pltpu.CompilerParams(
            collective_id=1, has_side_effects=True, vmem_limit_bytes=63 * 1024 * 1024
        ),
        name="forget_ring",
    )(
        tokens, target, gate, up, down, proj_in.T, proj_out.T,
        segment_ids.reshape(1, count), queries,
    ).T


def pair_call(n, tokens, target, gate, up, down, proj_in, proj_out, segment_ids, queries):
    width, units = gate.shape
    half = units // 2
    rank = proj_in.shape[1]
    pieces = width // LANES
    rows = pieces // CHUNKS
    any_spec = pl.BlockSpec(memory_space=pl.ANY)
    vmem_spec = pl.BlockSpec(memory_space=pltpu.VMEM)
    dma = pltpu.SemaphoreType.DMA
    return pl.pallas_call(
        functools.partial(pair_kernel, n),
        out_shape=jax.ShapeDtypeStruct((SEQS, queries.shape[0]), F32),
        in_specs=[any_spec] * 9,
        out_specs=vmem_spec,
        scratch_shapes=[
            pltpu.VMEM((width, units), BF16),
            pltpu.VMEM((half + ROWS, width), BF16),
            pltpu.VMEM((rank, half), BF16),
            pltpu.VMEM((rank, width), BF16),
            pltpu.VMEM((1, width), BF16),
            pltpu.VMEM((1, width), BF16),
            pltpu.VMEM(queries.shape, BF16),
            pltpu.VMEM((pieces, LANES), F32),
            pltpu.VMEM((pieces, LANES), BF16),
            pltpu.VMEM((CHUNKS, 2 * n, rows, LANES), BF16),
            pltpu.VMEM((max(2 * n * rows, half // LANES * rank), LANES), F32),
            pltpu.VMEM((2 * n, width // CHUNKS), BF16),
            pltpu.SMEM((n,), jnp.int32),
            pltpu.VMEM((2 * n, units), F32),
            pltpu.VMEM((rank, half + ROWS), F32),
            pltpu.VMEM((4 * rank, half + ROWS), BF16),
            pltpu.VMEM((2, n, LANES), F32),
            pltpu.VMEM((n, LANES), F32),
            pltpu.VMEM((n, LANES), F32),
            pltpu.VMEM((n, n, LANES), F32),
            pltpu.VMEM((LANES, LANES), F32),
            dma((FINE,)),
            dma((FINE,)),
            dma((FINE,)),
            dma((6,)),
            dma((CHUNKS,)),
            dma((CHUNKS,)),
            dma((CHUNKS,)),
            dma((CHUNKS,)),
            dma,
            dma,
            dma((n,)),
            dma((n,)),
        ],
        compiler_params=pltpu.CompilerParams(
            collective_id=0, has_side_effects=True, vmem_limit_bytes=63 * 1024 * 1024
        ),
        name="forget_pair",
    )(tokens, target, gate, up, down, proj_in.T, proj_out.T, segment_ids, queries).T


def solution(mesh):
    n = mesh.shape["query"]
    groups = mesh.shape["groups"]

    def local(tokens, target, gate, up, down, proj_in, proj_out, segment_ids, queries):
        width, units = gate.shape
        shared = (
            groups == 2
            and n == 16
            and segment_ids.shape[0] == n
            and tokens.shape[0] == 1
            and units % (2 * LANES) == 0
            and width % (FINE * LANES) == 0
            and 2 * proj_in.shape[1] == LANES
        )
        call = pair_call if shared else ring_call
        return call(n, tokens, target, gate, up, down, proj_in, proj_out, segment_ids, queries)

    in_specs = (
        P(("groups", "query"), None),
        P(("groups", "query"), None),
        P(None, "query"),
        P(None, "query"),
        P("query", None),
        P("query", None),
        P(),
        P("groups"),
        P("query", None),
    )
    return jax.shard_map(
        local, mesh=mesh, in_specs=in_specs, out_specs=P("query", "groups"), check_vma=False
    )
```

```python
import functools

import jax
import jax.numpy as jnp
from jax import lax
from jax.experimental import pallas as pl
from jax.experimental.pallas import tpu as pltpu
from jax.sharding import PartitionSpec as P

SEQS = 4
DEPTH = 1024
SLOTS = 5
DOWN_SLOTS = 4
CHUNKS = 4
FINE = 8
STEPS = 4
ROWS = 16
LANES = 128
F32 = jnp.float32
BF16 = jnp.bfloat16
MESH = pl.DeviceIdType.MESH


def split(value):
    high = value.astype(BF16)
    return high, (value - high.astype(F32)).astype(BF16)


def dot(a, b):
    return jnp.dot(a, b, preferred_element_type=F32)


def dot_lanes(a, b):
    return lax.dot_general(a, b, (((1,), (1,)), ((), ())), preferred_element_type=F32)


def pack(value):
    half = value.shape[0] // 2
    return jnp.concatenate([value[:half], value[half:]], axis=1)


def ring_kernel(
    n, tokens, target, gate, up, down, proj_in, proj_out, segment_ids, queries, scores,
    gate_ring, up_ring, down_ring, pin, pout, tok, tgt, qbuf, slab32, slab, gathered, x32, x16,
    expand, spread, gate_acc, up_acc, hidden_ref, block, side_acc, payload_a, payload_b, parts_a, parts_b,
    gate_sem, up_sem, down_sem, load_sem, tok_send, tok_recv, a_send, a_recv, b_send, b_recv,
):
    me = lax.axis_index("query")
    width = gate.shape[0]
    rank = proj_in.shape[0]
    count = x16.shape[0]
    pieces = width // LANES
    steps = width // DEPTH
    slots = gate_ring.shape[0]
    down_slots = down_ring.shape[0]

    def peer(d):
        return lax.rem(me + d, n)

    barrier = pltpu.get_barrier_semaphore()

    @pl.loop(1, n)
    def _(d):
        pl.semaphore_signal(barrier, inc=1, device_id={"query": peer(d)}, device_id_type=MESH)

    loads = [
        pltpu.make_async_copy(src, dst, load_sem.at[i])
        for i, (src, dst) in enumerate(
            [(tokens, tok), (target, tgt), (proj_out, pout), (proj_in, pin), (queries, qbuf)]
        )
    ]

    def chunk(c):
        return pl.ds(pl.multiple_of(c * DEPTH, DEPTH), DEPTH)

    def ring_copies(c, slot):
        return (
            pltpu.make_async_copy(gate.at[chunk(c), :], gate_ring.at[slot], gate_sem.at[slot]),
            pltpu.make_async_copy(up.at[chunk(c), :], up_ring.at[slot], up_sem.at[slot]),
        )

    def down_copy(c):
        slot = lax.rem(c, down_slots)
        return pltpu.make_async_copy(down.at[:, chunk(c)], down_ring.at[slot], down_sem.at[slot])

    for load in loads[:3]:
        load.start()
    for c in range(slots):
        for copy in ring_copies(c, c):
            copy.start()
    loads[3].start()
    loads[4].start()

    loads[0].wait()
    for k in range(pieces):
        slab32[k : k + 1, :] = tok[:, k * LANES : (k + 1) * LANES].astype(F32)
    slab[...] = slab32[...].astype(BF16)
    gathered[me] = slab[...]

    pl.semaphore_wait(barrier, n - 1)

    def push(src, dst, send, recv, d, slot):
        return pltpu.make_async_remote_copy(
            src_ref=src,
            dst_ref=dst.at[slot],
            send_sem=send.at[d],
            recv_sem=recv.at[slot],
            device_id={"query": peer(d)},
            device_id_type=MESH,
        )

    token_push = functools.partial(push, slab, gathered, tok_send, tok_recv)
    a_push = functools.partial(push, payload_a, parts_a, a_send, a_recv)
    b_push = functools.partial(push, payload_b, parts_b, b_send, b_recv)

    def start_all(copy):
        @pl.loop(1, n)
        def _(d):
            copy(d, me).start()

    def receive_all(copy):
        @pl.loop(1, n)
        def _(d):
            copy(d, peer(d)).wait_recv()

    start_all(token_push)

    owner = lax.broadcasted_iota(jnp.int32, expand.shape, 1) // rank
    expand[...] = jnp.where(
        lax.broadcasted_iota(jnp.int32, expand.shape, 0) == owner, 1.0, 0.0
    ).astype(BF16)
    gate_acc[...] = jnp.zeros_like(gate_acc)
    up_acc[...] = jnp.zeros_like(up_acc)
    side_acc[...] = jnp.zeros_like(side_acc)
    loads[1].wait()
    loads[2].wait()
    target_side = dot_lanes(tgt[...], pout[...])

    receive_all(token_push)
    x32[...] = gathered[...].reshape(n * pieces, LANES).astype(F32)
    for k in range(pieces):
        x16[:, k * LANES : (k + 1) * LANES] = x32[pl.ds(k, n, stride=pieces), :].astype(BF16)

    @pl.loop(0, steps)
    def _(c):
        slot = lax.rem(c, slots)
        for copy in ring_copies(c, slot):
            copy.wait()
        x = x16[:, chunk(c)]
        gate_acc[...] += dot(x, gate_ring[slot])
        up_acc[...] += dot(x, up_ring[slot])

        @pl.when(c + slots < steps)
        def _():
            for copy in ring_copies(c + slots, slot):
                copy.start()

        @pl.when(c < down_slots)
        def _():
            down_copy(c).start()

    gate_pre = gate_acc[...]
    hidden = (gate_pre / (1.0 + jnp.exp(-gate_pre)) * up_acc[...]).astype(BF16)
    hidden_ref[...] = hidden
    loads[3].wait()
    payload_a[...] = pack(dot_lanes(hidden, pin[...]))
    start_all(a_push)
    parts_a[me] = payload_a[...]

    def down_dot(c):
        down_copy(c).wait()
        high, low = split(dot(hidden_ref[...], down_ring[lax.rem(c, down_slots)]))
        return jnp.concatenate([high, low], axis=0)

    def project(c):
        side_acc[...] += dot_lanes(block[...], pout[:, chunk(c)])

    def refill(c):
        @pl.when(c + down_slots < steps)
        def _():
            down_copy(c + down_slots).start()

    block[...] = down_dot(0)
    refill(0)

    @pl.loop(1, steps)
    def _(c):
        new = down_dot(c)
        project(c - 1)
        block[...] = new
        refill(c)

    project(steps - 1)

    def sum_parts(parts):
        return lax.fori_loop(
            0, n, lambda p, t: t + parts[p], jnp.zeros(parts.shape[1:], F32), unroll=8
        )

    side = side_acc[:count, :] + side_acc[count:, :]
    own_row = lax.broadcasted_iota(jnp.int32, side.shape, 0) == me
    side = side - jnp.where(own_row, jnp.broadcast_to(target_side, side.shape), 0.0)
    payload_b[...] = pack(side)
    start_all(b_push)
    parts_b[me] = payload_b[...]
    segments = jnp.concatenate([segment_ids[...], segment_ids[...]], axis=1)
    marks = (
        lax.broadcasted_iota(jnp.int32, (2 * SEQS, 2 * count), 0) == segments
    ).astype(BF16)

    receive_all(a_push)
    total = sum_parts(parts_a)
    input_side = jnp.concatenate([total[:, :rank], total[:, rank:]], axis=0)
    high, low = split(input_side)
    wide = dot(jnp.concatenate([high, low], axis=0), expand[...])
    spread[...] = wide[:count] + wide[count:]
    loads[4].wait()

    @pl.loop(1, n)
    def _(d):
        token_push(d, me).wait_send()
        a_push(d, me).wait_send()
        b_push(d, me).wait_send()

    receive_all(b_push)
    total = sum_parts(parts_b)
    first, second = total[:, :rank], total[:, rank:]
    doubled = jnp.concatenate(
        [jnp.concatenate([first, first], axis=1), jnp.concatenate([second, second], axis=1)],
        axis=0,
    )
    pairs = spread[...] * jnp.concatenate([doubled] * (rank // 2), axis=1)
    high, low = split(pairs)
    kronecker = dot(marks, jnp.concatenate([high, low], axis=0))
    scores[...] = dot_lanes(kronecker.astype(BF16), qbuf[...])[:SEQS]


def pair_kernel(
    n, tokens, target, gate, up, down, proj_in, proj_out, segment_ids, queries, scores,
    both_v, down_v, pin, pout, tok, tgt, qbuf, slab32, slab, gathered, x32, x16, ids,
    both_acc, side_t, factors, payload, sibling_part, reduced, parts, kron,
    gate_sem, up_sem, down_sem, load_sem, tok_send, tok_recv, fwd_send, fwd_recv,
    pre_send, pre_recv, part_send, part_recv,
):
    g = lax.axis_index("groups")
    me = lax.axis_index("query")
    core = lax.rem(me, 2)
    sibling = me + 1 - 2 * core
    columns = n // 2
    chips = 2 * columns
    chip = g * columns + lax.div(me, 2)
    own = core * chips + chip
    width = gate.shape[0]
    half = both_v.shape[1] // 2
    rank = proj_in.shape[0]
    chunks = gathered.shape[0]
    rows = gathered.shape[2]
    span = width // chunks
    fine = gate_sem.shape[0]
    step = width // fine
    per = fine // chunks

    barrier = pltpu.get_barrier_semaphore()

    def peer(d):
        other = lax.rem(chip + d, chips)
        return lax.div(other, columns), 2 * lax.rem(other, columns) + core

    order = sorted(range(1, chips), key=lambda d: abs(d % columns - columns // 2))
    for d in order:
        pl.semaphore_signal(barrier, inc=1, device_id=peer(d), device_id_type=MESH)
    pl.semaphore_signal(barrier, inc=1, device_id=(g, sibling), device_id_type=MESH)

    units = pl.ds(pl.multiple_of(g * half, LANES), half)

    def cut(c):
        return pl.ds(pl.multiple_of(c * step, step), step)

    loads = [
        pltpu.make_async_copy(src, dst, load_sem.at[i])
        for i, (src, dst) in enumerate(
            [
                (tokens, tok), (proj_out, pout), (target, tgt),
                (proj_in.at[:, units], pin), (queries, qbuf), (segment_ids, ids),
            ]
        )
    ]

    def down_copy(c):
        return pltpu.make_async_copy(down.at[units, cut(c)], down_v.at[:half, cut(c)], down_sem.at[c])

    def gate_copies(c):
        return (
            pltpu.make_async_copy(gate.at[cut(c), units], both_v.at[cut(c), :half], gate_sem.at[c]),
            pltpu.make_async_copy(up.at[cut(c), units], both_v.at[cut(c), half:], up_sem.at[c]),
        )

    for load in loads[:4]:
        load.start()

    @pl.loop(0, fine)
    def _(c):
        down_copy(c).start()

    @pl.loop(0, fine)
    def _(c):
        for copy in gate_copies(c):
            copy.start()

    for load in loads[4:]:
        load.start()

    loads[0].wait()
    for k in range(width // LANES):
        slab32[k : k + 1, :] = tok[:, k * LANES : (k + 1) * LANES].astype(F32)
    slab[...] = slab32[...].astype(BF16)
    for c in range(chunks):
        gathered[c, own] = slab[c * rows : (c + 1) * rows, :]

    def token_push(c, d, slot):
        return pltpu.make_async_remote_copy(
            src_ref=slab.at[pl.ds(pl.multiple_of(c * rows, rows), rows), :],
            dst_ref=gathered.at[c, slot],
            send_sem=tok_send.at[c],
            recv_sem=tok_recv.at[c],
            device_id=peer(d),
            device_id_type=MESH,
        )

    def forward(c, owner):
        block = gathered.at[c, pl.ds(owner * chips, chips)]
        return pltpu.make_async_remote_copy(
            src_ref=block, dst_ref=block, send_sem=fwd_send.at[c], recv_sem=fwd_recv.at[c],
            device_id=(g, sibling), device_id_type=MESH,
        )

    both_acc[...] = jnp.zeros_like(both_acc)
    side_t[...] = jnp.zeros_like(side_t)
    loads[2].wait()
    top = lax.broadcasted_iota(jnp.int32, (ROWS, width), 0) == 0
    down_v[half:, :] = jnp.where(
        top, jnp.broadcast_to(tgt[...].astype(F32), top.shape), 0.0
    ).astype(BF16)
    loads[1].wait()

    wide = width // STEPS

    def project(c):
        here = pl.ds(pl.multiple_of(c * wide, wide), wide)
        for i in range(fine // STEPS):
            down_copy(c * (fine // STEPS) + i).wait()
        side_t[...] += dot_lanes(pout[:, here], down_v[:, here])

    def push_chunk(c):
        for d in order:
            token_push(c, d, own).start()

    project(0)
    pl.semaphore_wait(barrier, chips)
    push_chunk(0)

    @pl.loop(1, STEPS)
    def _(c):
        push_chunk(c)
        project(c)

    high, low = split(side_t[...])
    factors[0:rank, half:] = jnp.zeros((rank, ROWS), BF16)
    factors[rank : 2 * rank, :] = high
    factors[2 * rank : 3 * rank, :] = jnp.zeros_like(high)
    factors[3 * rank : 4 * rank, :] = low
    loads[3].wait()
    for k in range(half // LANES):
        lanes = slice(k * LANES, (k + 1) * LANES)
        x32[k * rank : (k + 1) * rank, :] = pin[:, lanes].astype(F32)
        for parity in range(2):
            factors[parity * (rank // 2) : (parity + 1) * (rank // 2), lanes] = x32[
                pl.ds(k * rank + parity, rank // 2, stride=2), :
            ].astype(BF16)

    def all_chips(c, semaphore):
        others = gathered.at[c, pl.ds(0, chips - 1)]
        return pltpu.make_async_copy(others, others, semaphore.at[c])

    def relay(c):
        all_chips(c, tok_recv).wait()
        forward(c, core).start()

    def convert(first, last):
        for k in range(first, last):
            x16[:, k * LANES : (k + 1) * LANES] = x32[pl.ds(k, 2 * n, stride=rows), :].astype(BF16)

    relay(0)
    relay(1)

    @pl.loop(0, chunks)
    def _(c):
        for i in range(per):
            for copy in gate_copies(c * per + i):
                copy.wait()
        forward(c, 1 - core).wait_recv()
        x32[0 : 2 * n * rows, :] = gathered[c].reshape(2 * n * rows, LANES).astype(F32)
        convert(0, rows)
        here = pl.ds(pl.multiple_of(c * span, span), span)
        both_acc[:, :half] += dot(x16[...], both_v[here, :half])
        both_acc[:, half:] += dot(x16[...], both_v[here, half:])

        @pl.when(c + 2 < chunks)
        def _():
            relay(c + 2)

    gate_pre = both_acc[:, :half]
    hidden = (gate_pre / (1.0 + jnp.exp(-gate_pre)) * both_acc[:, half:]).astype(BF16)
    shape = (2 * n, ROWS)
    own_target = (lax.broadcasted_iota(jnp.int32, shape, 0) == own) & (
        lax.broadcasted_iota(jnp.int32, shape, 1) == 0
    )
    sides = dot_lanes(
        jnp.concatenate([hidden, jnp.where(own_target, -1.0, 0.0).astype(BF16)], axis=1), factors[...]
    )
    sides = sides[:, :LANES] + sides[:, LANES:]
    eight = columns
    for k in range(2):
        payload[k, :eight] = sides[k * eight : (k + 1) * eight]
        payload[k, eight:] = sides[chips + k * eight : chips + (k + 1) * eight]

    merge = pltpu.make_async_remote_copy(
        src_ref=payload.at[1 - core], dst_ref=sibling_part, send_sem=pre_send, recv_sem=pre_recv,
        device_id=(g, sibling), device_id_type=MESH,
    )
    merge.start()

    loads[5].wait()
    segment_row = lax.broadcasted_iota(jnp.int32, (n, LANES), 0)
    segment_of = jnp.zeros((n, LANES), jnp.int32)
    for t in range(n):
        segment_of = jnp.where(
            segment_row == (t % 2) * columns + t // 2, ids[t], segment_of
        )
    lane = lax.broadcasted_iota(jnp.int32, (n, LANES), 1)
    quarter = lane // (LANES // SEQS)
    member = quarter == segment_of

    merge.wait_recv()
    total = payload[core] + sibling_part[...]
    reduced[...] = total

    def part_push(d):
        return pltpu.make_async_remote_copy(
            src_ref=reduced, dst_ref=parts.at[chip], send_sem=part_send, recv_sem=part_recv,
            device_id=(core, lax.rem(me + d, n)), device_id_type=MESH,
        )

    def all_parts(count, semaphore):
        some = parts.at[pl.ds(0, count)]
        pltpu.make_async_copy(some, some, semaphore).wait()

    for d in range(1, n):
        part_push(d).start()

    @pl.when(core != g)
    def _():
        part_push(0).start()

    @pl.when(core == g)
    def _():
        parts[chip] = reduced[...]

    merge.wait_send()

    @pl.loop(0, chunks)
    def _(c):
        all_chips(c, tok_send).wait()
        forward(c, core).wait_send()

    loads[4].wait()

    for semaphore in (part_send, part_recv):

        @pl.when(core == g)
        def _():
            all_parts(chips - 1, semaphore)

        @pl.when(core != g)
        def _():
            all_parts(chips, semaphore)

    total = parts[0]
    for p in range(1, chips):
        total = total + parts[p]
    turned = [total] + [pltpu.roll(total, LANES // SEQS * k, axis=1) for k in range(1, SEQS)]

    def tiled(offset):
        out = turned[-offset % SEQS]
        for k in range(1, SEQS):
            out = jnp.where(quarter == k, turned[(k - offset) % SEQS], out)
        return jnp.where(member, out, 0.0)

    left = jnp.concatenate([tiled(0), tiled(1)], axis=0)
    both = jnp.where(lane < rank, turned[2], total)
    right = jnp.concatenate(
        [jnp.where(lane < rank, both, 0.0), jnp.where(lane < rank, 0.0, both)], axis=0
    )
    left_high, left_low = split(left)
    right_high, right_low = split(right)
    kron[...] = lax.dot_general(
        jnp.concatenate([left_high, left_low, left_high], axis=0),
        jnp.concatenate([right_high, right_high, right_low], axis=0),
        (((0,), (0,)), ((), ())),
        preferred_element_type=F32,
    )
    quarters = LANES // SEQS
    kronecker = jnp.concatenate(
        [kron[pl.ds(k, SEQS, stride=quarters), :] for k in range(quarters)], axis=1
    ).astype(BF16)
    scores[...] = dot_lanes(kronecker, qbuf[...])


def ring_call(n, tokens, target, gate, up, down, proj_in, proj_out, segment_ids, queries):
    width, units = gate.shape
    rank = proj_in.shape[1]
    count = segment_ids.shape[0]
    pieces = width // LANES
    any_spec = pl.BlockSpec(memory_space=pl.ANY)
    vmem_spec = pl.BlockSpec(memory_space=pltpu.VMEM)
    dma = pltpu.SemaphoreType.DMA
    return pl.pallas_call(
        functools.partial(ring_kernel, n),
        out_shape=jax.ShapeDtypeStruct((SEQS, queries.shape[0]), F32),
        in_specs=[any_spec] * 7 + [vmem_spec, any_spec],
        out_specs=vmem_spec,
        scratch_shapes=[
            pltpu.VMEM((SLOTS, DEPTH, units), BF16),
            pltpu.VMEM((SLOTS, DEPTH, units), BF16),
            pltpu.VMEM((DOWN_SLOTS, units, DEPTH), BF16),
            pltpu.VMEM((rank, units), BF16),
            pltpu.VMEM((rank, width), BF16),
            pltpu.VMEM((1, width), BF16),
            pltpu.VMEM((1, width), BF16),
            pltpu.VMEM(queries.shape, BF16),
            pltpu.VMEM((pieces, LANES), F32),
            pltpu.VMEM((pieces, LANES), BF16),
            pltpu.VMEM((n, pieces, LANES), BF16),
            pltpu.VMEM((n * pieces, LANES), F32),
            pltpu.VMEM((count, width), BF16),
            pltpu.VMEM((rank, rank * rank), BF16),
            pltpu.VMEM((count, rank * rank), F32),
            pltpu.VMEM((count, units), F32),
            pltpu.VMEM((count, units), F32),
            pltpu.VMEM((count, units), BF16),
            pltpu.VMEM((2 * count, DEPTH), BF16),
            pltpu.VMEM((2 * count, rank), F32),
            pltpu.VMEM((count // 2, 2 * rank), F32),
            pltpu.VMEM((count // 2, 2 * rank), F32),
            pltpu.VMEM((n, count // 2, 2 * rank), F32),
            pltpu.VMEM((n, count // 2, 2 * rank), F32),
            dma((SLOTS,)),
            dma((SLOTS,)),
            dma((DOWN_SLOTS,)),
            dma((5,)),
            dma((n,)),
            dma((n,)),
            dma((n,)),
            dma((n,)),
            dma((n,)),
            dma((n,)),
        ],
        compiler_params=pltpu.CompilerParams(
            collective_id=1, has_side_effects=True, vmem_limit_bytes=63 * 1024 * 1024
        ),
        name="forget_ring",
    )(
        tokens, target, gate, up, down, proj_in.T, proj_out.T,
        segment_ids.reshape(1, count), queries,
    ).T


def pair_call(n, tokens, target, gate, up, down, proj_in, proj_out, segment_ids, queries):
    width, units = gate.shape
    half = units // 2
    rank = proj_in.shape[1]
    pieces = width // LANES
    rows = pieces // CHUNKS
    any_spec = pl.BlockSpec(memory_space=pl.ANY)
    vmem_spec = pl.BlockSpec(memory_space=pltpu.VMEM)
    dma = pltpu.SemaphoreType.DMA
    return pl.pallas_call(
        functools.partial(pair_kernel, n),
        out_shape=jax.ShapeDtypeStruct((SEQS, queries.shape[0]), F32),
        in_specs=[any_spec] * 9,
        out_specs=vmem_spec,
        scratch_shapes=[
            pltpu.VMEM((width, units), BF16),
            pltpu.VMEM((half + ROWS, width), BF16),
            pltpu.VMEM((rank, half), BF16),
            pltpu.VMEM((rank, width), BF16),
            pltpu.VMEM((1, width), BF16),
            pltpu.VMEM((1, width), BF16),
            pltpu.VMEM(queries.shape, BF16),
            pltpu.VMEM((pieces, LANES), F32),
            pltpu.VMEM((pieces, LANES), BF16),
            pltpu.VMEM((CHUNKS, 2 * n, rows, LANES), BF16),
            pltpu.VMEM((max(2 * n * rows, half // LANES * rank), LANES), F32),
            pltpu.VMEM((2 * n, width // CHUNKS), BF16),
            pltpu.SMEM((n,), jnp.int32),
            pltpu.VMEM((2 * n, units), F32),
            pltpu.VMEM((rank, half + ROWS), F32),
            pltpu.VMEM((4 * rank, half + ROWS), BF16),
            pltpu.VMEM((2, n, LANES), F32),
            pltpu.VMEM((n, LANES), F32),
            pltpu.VMEM((n, LANES), F32),
            pltpu.VMEM((n, n, LANES), F32),
            pltpu.VMEM((LANES, LANES), F32),
            dma((FINE,)),
            dma((FINE,)),
            dma((FINE,)),
            dma((6,)),
            dma((CHUNKS,)),
            dma((CHUNKS,)),
            dma((CHUNKS,)),
            dma((CHUNKS,)),
            dma,
            dma,
            dma,
            dma,
        ],
        compiler_params=pltpu.CompilerParams(
            collective_id=0, has_side_effects=True, vmem_limit_bytes=63 * 1024 * 1024
        ),
        name="forget_pair",
    )(tokens, target, gate, up, down, proj_in.T, proj_out.T, segment_ids, queries).T


def solution(mesh):
    n = mesh.shape["query"]
    groups = mesh.shape["groups"]

    def local(tokens, target, gate, up, down, proj_in, proj_out, segment_ids, queries):
        width, units = gate.shape
        shared = (
            groups == 2
            and n == 16
            and segment_ids.shape[0] == n
            and tokens.shape[0] == 1
            and units % (2 * LANES) == 0
            and width % (FINE * LANES) == 0
            and 2 * proj_in.shape[1] == LANES
        )
        call = pair_call if shared else ring_call
        return call(n, tokens, target, gate, up, down, proj_in, proj_out, segment_ids, queries)

    in_specs = (
        P(("groups", "query"), None),
        P(("groups", "query"), None),
        P(None, "query"),
        P(None, "query"),
        P("query", None),
        P("query", None),
        P(),
        P("groups"),
        P("query", None),
    )
    return jax.shard_map(
        local, mesh=mesh, in_specs=in_specs, out_specs=P("query", "groups"), check_vma=False
    )
```

```python
import functools

import jax
import jax.numpy as jnp
from jax import lax
from jax.experimental import pallas as pl
from jax.experimental.pallas import tpu as pltpu
from jax.sharding import PartitionSpec as P

SEQS = 4
DEPTH = 1024
SLOTS = 5
DOWN_SLOTS = 4
CHUNKS = 4
FINE = 8
STEPS = 4
ROWS = 16
LANES = 128
F32 = jnp.float32
BF16 = jnp.bfloat16
MESH = pl.DeviceIdType.MESH


def split(value):
    high = value.astype(BF16)
    return high, (value - high.astype(F32)).astype(BF16)


def dot(a, b):
    return jnp.dot(a, b, preferred_element_type=F32)


def dot_lanes(a, b):
    return lax.dot_general(a, b, (((1,), (1,)), ((), ())), preferred_element_type=F32)


def pack(value):
    half = value.shape[0] // 2
    return jnp.concatenate([value[:half], value[half:]], axis=1)


def ring_kernel(
    n, tokens, target, gate, up, down, proj_in, proj_out, segment_ids, queries, scores,
    gate_ring, up_ring, down_ring, pin, pout, tok, tgt, qbuf, slab32, slab, gathered, x32, x16,
    expand, spread, gate_acc, up_acc, hidden_ref, block, side_acc, payload_a, payload_b, parts_a, parts_b,
    gate_sem, up_sem, down_sem, load_sem, tok_send, tok_recv, a_send, a_recv, b_send, b_recv,
):
    me = lax.axis_index("query")
    width = gate.shape[0]
    rank = proj_in.shape[0]
    count = x16.shape[0]
    pieces = width // LANES
    steps = width // DEPTH
    slots = gate_ring.shape[0]
    down_slots = down_ring.shape[0]

    def peer(d):
        return lax.rem(me + d, n)

    barrier = pltpu.get_barrier_semaphore()

    @pl.loop(1, n)
    def _(d):
        pl.semaphore_signal(barrier, inc=1, device_id={"query": peer(d)}, device_id_type=MESH)

    loads = [
        pltpu.make_async_copy(src, dst, load_sem.at[i])
        for i, (src, dst) in enumerate(
            [(tokens, tok), (target, tgt), (proj_out, pout), (proj_in, pin), (queries, qbuf)]
        )
    ]

    def chunk(c):
        return pl.ds(pl.multiple_of(c * DEPTH, DEPTH), DEPTH)

    def ring_copies(c, slot):
        return (
            pltpu.make_async_copy(gate.at[chunk(c), :], gate_ring.at[slot], gate_sem.at[slot]),
            pltpu.make_async_copy(up.at[chunk(c), :], up_ring.at[slot], up_sem.at[slot]),
        )

    def down_copy(c):
        slot = lax.rem(c, down_slots)
        return pltpu.make_async_copy(down.at[:, chunk(c)], down_ring.at[slot], down_sem.at[slot])

    for load in loads[:3]:
        load.start()
    for c in range(slots):
        for copy in ring_copies(c, c):
            copy.start()
    loads[3].start()
    loads[4].start()

    loads[0].wait()
    for k in range(pieces):
        slab32[k : k + 1, :] = tok[:, k * LANES : (k + 1) * LANES].astype(F32)
    slab[...] = slab32[...].astype(BF16)
    gathered[me] = slab[...]

    pl.semaphore_wait(barrier, n - 1)

    def push(src, dst, send, recv, d, slot):
        return pltpu.make_async_remote_copy(
            src_ref=src,
            dst_ref=dst.at[slot],
            send_sem=send.at[d],
            recv_sem=recv.at[slot],
            device_id={"query": peer(d)},
            device_id_type=MESH,
        )

    token_push = functools.partial(push, slab, gathered, tok_send, tok_recv)
    a_push = functools.partial(push, payload_a, parts_a, a_send, a_recv)
    b_push = functools.partial(push, payload_b, parts_b, b_send, b_recv)

    def start_all(copy):
        @pl.loop(1, n)
        def _(d):
            copy(d, me).start()

    def receive_all(copy):
        @pl.loop(1, n)
        def _(d):
            copy(d, peer(d)).wait_recv()

    start_all(token_push)

    owner = lax.broadcasted_iota(jnp.int32, expand.shape, 1) // rank
    expand[...] = jnp.where(
        lax.broadcasted_iota(jnp.int32, expand.shape, 0) == owner, 1.0, 0.0
    ).astype(BF16)
    gate_acc[...] = jnp.zeros_like(gate_acc)
    up_acc[...] = jnp.zeros_like(up_acc)
    side_acc[...] = jnp.zeros_like(side_acc)
    loads[1].wait()
    loads[2].wait()
    target_side = dot_lanes(tgt[...], pout[...])

    receive_all(token_push)
    x32[...] = gathered[...].reshape(n * pieces, LANES).astype(F32)
    for k in range(pieces):
        x16[:, k * LANES : (k + 1) * LANES] = x32[pl.ds(k, n, stride=pieces), :].astype(BF16)

    @pl.loop(0, steps)
    def _(c):
        slot = lax.rem(c, slots)
        for copy in ring_copies(c, slot):
            copy.wait()
        x = x16[:, chunk(c)]
        gate_acc[...] += dot(x, gate_ring[slot])
        up_acc[...] += dot(x, up_ring[slot])

        @pl.when(c + slots < steps)
        def _():
            for copy in ring_copies(c + slots, slot):
                copy.start()

        @pl.when(c < down_slots)
        def _():
            down_copy(c).start()

    gate_pre = gate_acc[...]
    hidden = (gate_pre / (1.0 + jnp.exp(-gate_pre)) * up_acc[...]).astype(BF16)
    hidden_ref[...] = hidden
    loads[3].wait()
    payload_a[...] = pack(dot_lanes(hidden, pin[...]))
    start_all(a_push)
    parts_a[me] = payload_a[...]

    def down_dot(c):
        down_copy(c).wait()
        high, low = split(dot(hidden_ref[...], down_ring[lax.rem(c, down_slots)]))
        return jnp.concatenate([high, low], axis=0)

    def project(c):
        side_acc[...] += dot_lanes(block[...], pout[:, chunk(c)])

    def refill(c):
        @pl.when(c + down_slots < steps)
        def _():
            down_copy(c + down_slots).start()

    block[...] = down_dot(0)
    refill(0)

    @pl.loop(1, steps)
    def _(c):
        new = down_dot(c)
        project(c - 1)
        block[...] = new
        refill(c)

    project(steps - 1)

    def sum_parts(parts):
        return lax.fori_loop(
            0, n, lambda p, t: t + parts[p], jnp.zeros(parts.shape[1:], F32), unroll=8
        )

    side = side_acc[:count, :] + side_acc[count:, :]
    own_row = lax.broadcasted_iota(jnp.int32, side.shape, 0) == me
    side = side - jnp.where(own_row, jnp.broadcast_to(target_side, side.shape), 0.0)
    payload_b[...] = pack(side)
    start_all(b_push)
    parts_b[me] = payload_b[...]
    segments = jnp.concatenate([segment_ids[...], segment_ids[...]], axis=1)
    marks = (
        lax.broadcasted_iota(jnp.int32, (2 * SEQS, 2 * count), 0) == segments
    ).astype(BF16)

    receive_all(a_push)
    total = sum_parts(parts_a)
    input_side = jnp.concatenate([total[:, :rank], total[:, rank:]], axis=0)
    high, low = split(input_side)
    wide = dot(jnp.concatenate([high, low], axis=0), expand[...])
    spread[...] = wide[:count] + wide[count:]
    loads[4].wait()

    @pl.loop(1, n)
    def _(d):
        token_push(d, me).wait_send()
        a_push(d, me).wait_send()
        b_push(d, me).wait_send()

    receive_all(b_push)
    total = sum_parts(parts_b)
    first, second = total[:, :rank], total[:, rank:]
    doubled = jnp.concatenate(
        [jnp.concatenate([first, first], axis=1), jnp.concatenate([second, second], axis=1)],
        axis=0,
    )
    pairs = spread[...] * jnp.concatenate([doubled] * (rank // 2), axis=1)
    high, low = split(pairs)
    kronecker = dot(marks, jnp.concatenate([high, low], axis=0))
    scores[...] = dot_lanes(kronecker.astype(BF16), qbuf[...])[:SEQS]


def pair_kernel(
    n, tokens, target, gate, up, down, proj_in, proj_out, segment_ids, queries, scores,
    both_v, down_v, pin, pout, tok, tgt, qbuf, slab32, slab, gathered, x32, x16, ids,
    both_acc, side_t, factors, payload, sibling_part, reduced, parts, kron,
    gate_sem, up_sem, down_sem, load_sem, tok_send, tok_recv, fwd_send, fwd_recv,
    pre_send, pre_recv, part_send, part_recv,
):
    g = lax.axis_index("groups")
    me = lax.axis_index("query")
    core = lax.rem(me, 2)
    sibling = me + 1 - 2 * core
    columns = n // 2
    chips = 2 * columns
    chip = g * columns + lax.div(me, 2)
    own = core * chips + chip
    width = gate.shape[0]
    half = both_v.shape[1] // 2
    rank = proj_in.shape[0]
    chunks = gathered.shape[0]
    rows = gathered.shape[2]
    span = width // chunks
    fine = gate_sem.shape[0]
    step = width // fine
    per = fine // chunks

    barrier = pltpu.get_barrier_semaphore()

    def peer(d):
        other = lax.rem(chip + d, chips)
        return lax.div(other, columns), 2 * lax.rem(other, columns) + core

    order = sorted(range(1, chips), key=lambda d: abs(d % columns - columns // 2))
    for d in order:
        pl.semaphore_signal(barrier, inc=1, device_id=peer(d), device_id_type=MESH)
    pl.semaphore_signal(barrier, inc=1, device_id=(g, sibling), device_id_type=MESH)

    units = pl.ds(pl.multiple_of(g * half, LANES), half)

    def cut(c):
        return pl.ds(pl.multiple_of(c * step, step), step)

    loads = [
        pltpu.make_async_copy(src, dst, load_sem.at[i])
        for i, (src, dst) in enumerate(
            [
                (tokens, tok), (proj_out, pout), (target, tgt),
                (proj_in.at[:, units], pin), (queries, qbuf), (segment_ids, ids),
            ]
        )
    ]

    def down_copy(c):
        return pltpu.make_async_copy(down.at[units, cut(c)], down_v.at[:half, cut(c)], down_sem.at[c])

    def gate_copies(c):
        return (
            pltpu.make_async_copy(gate.at[cut(c), units], both_v.at[cut(c), :half], gate_sem.at[c]),
            pltpu.make_async_copy(up.at[cut(c), units], both_v.at[cut(c), half:], up_sem.at[c]),
        )

    for load in loads[:4]:
        load.start()

    @pl.loop(0, fine)
    def _(c):
        down_copy(c).start()

    @pl.loop(0, fine)
    def _(c):
        for copy in gate_copies(c):
            copy.start()

    for load in loads[4:]:
        load.start()

    loads[0].wait()
    for k in range(width // LANES):
        slab32[k : k + 1, :] = tok[:, k * LANES : (k + 1) * LANES].astype(F32)
    slab[...] = slab32[...].astype(BF16)
    for c in range(chunks):
        gathered[c, own] = slab[c * rows : (c + 1) * rows, :]

    def token_push(c, d, slot):
        return pltpu.make_async_remote_copy(
            src_ref=slab.at[pl.ds(pl.multiple_of(c * rows, rows), rows), :],
            dst_ref=gathered.at[c, slot],
            send_sem=tok_send.at[c],
            recv_sem=tok_recv.at[c],
            device_id=peer(d),
            device_id_type=MESH,
        )

    def forward(c, owner):
        block = gathered.at[c, pl.ds(owner * chips, chips)]
        return pltpu.make_async_remote_copy(
            src_ref=block, dst_ref=block, send_sem=fwd_send.at[c], recv_sem=fwd_recv.at[c],
            device_id=(g, sibling), device_id_type=MESH,
        )

    both_acc[...] = jnp.zeros_like(both_acc)
    side_t[...] = jnp.zeros_like(side_t)
    loads[2].wait()
    top = lax.broadcasted_iota(jnp.int32, (ROWS, width), 0) == 0
    down_v[half:, :] = jnp.where(
        top, jnp.broadcast_to(tgt[...].astype(F32), top.shape), 0.0
    ).astype(BF16)
    loads[1].wait()

    wide = width // STEPS

    def project(c):
        here = pl.ds(pl.multiple_of(c * wide, wide), wide)
        for i in range(fine // STEPS):
            down_copy(c * (fine // STEPS) + i).wait()
        side_t[...] += dot_lanes(pout[:, here], down_v[:, here])

    def push_chunk(c):
        for d in order:
            token_push(c, d, own).start()

    project(0)
    pl.semaphore_wait(barrier, chips)
    push_chunk(0)

    @pl.loop(1, STEPS)
    def _(c):
        push_chunk(c)
        project(c)

    high, low = split(side_t[...])
    factors[0:rank, half:] = jnp.zeros((rank, ROWS), BF16)
    factors[rank : 2 * rank, :] = high
    factors[2 * rank : 3 * rank, :] = jnp.zeros_like(high)
    factors[3 * rank : 4 * rank, :] = low
    loads[3].wait()
    for k in range(half // LANES):
        lanes = slice(k * LANES, (k + 1) * LANES)
        x32[k * rank : (k + 1) * rank, :] = pin[:, lanes].astype(F32)
        for parity in range(2):
            factors[parity * (rank // 2) : (parity + 1) * (rank // 2), lanes] = x32[
                pl.ds(k * rank + parity, rank // 2, stride=2), :
            ].astype(BF16)

    def all_chips(c, semaphore):
        others = gathered.at[c, pl.ds(0, chips - 1)]
        return pltpu.make_async_copy(others, others, semaphore.at[c])

    def relay(c):
        all_chips(c, tok_recv).wait()
        forward(c, core).start()

    def convert(first, last):
        for k in range(first, last):
            x16[:, k * LANES : (k + 1) * LANES] = x32[pl.ds(k, 2 * n, stride=rows), :].astype(BF16)

    relay(0)
    relay(1)

    @pl.loop(0, chunks)
    def _(c):
        for i in range(per):
            for copy in gate_copies(c * per + i):
                copy.wait()
        forward(c, 1 - core).wait_recv()
        x32[0 : 2 * n * rows, :] = gathered[c].reshape(2 * n * rows, LANES).astype(F32)
        convert(0, rows)
        here = pl.ds(pl.multiple_of(c * span, span), span)
        both_acc[:, :half] += dot(x16[...], both_v[here, :half])
        both_acc[:, half:] += dot(x16[...], both_v[here, half:])

        @pl.when(c + 2 < chunks)
        def _():
            relay(c + 2)

    gate_pre = both_acc[:, :half]
    hidden = (gate_pre / (1.0 + jnp.exp(-gate_pre)) * both_acc[:, half:]).astype(BF16)
    shape = (2 * n, ROWS)
    own_target = (lax.broadcasted_iota(jnp.int32, shape, 0) == own) & (
        lax.broadcasted_iota(jnp.int32, shape, 1) == 0
    )
    sides = dot_lanes(
        jnp.concatenate([hidden, jnp.where(own_target, -1.0, 0.0).astype(BF16)], axis=1), factors[...]
    )
    sides = sides[:, :LANES] + sides[:, LANES:]
    eight = columns
    for k in range(2):
        payload[k, :eight] = sides[k * eight : (k + 1) * eight]
        payload[k, eight:] = sides[chips + k * eight : chips + (k + 1) * eight]

    merge = pltpu.make_async_remote_copy(
        src_ref=payload.at[1 - core], dst_ref=sibling_part, send_sem=pre_send, recv_sem=pre_recv,
        device_id=(g, sibling), device_id_type=MESH,
    )
    merge.start()

    loads[5].wait()
    segment_row = lax.broadcasted_iota(jnp.int32, (n, LANES), 0)
    segment_of = jnp.zeros((n, LANES), jnp.int32)
    for t in range(n):
        segment_of = jnp.where(
            segment_row == (t % 2) * columns + t // 2, ids[t], segment_of
        )
    lane = lax.broadcasted_iota(jnp.int32, (n, LANES), 1)
    quarter = lane // (LANES // SEQS)
    member = quarter == segment_of

    merge.wait_recv()
    total = payload[core] + sibling_part[...]
    reduced[...] = total

    def part_push(d):
        return pltpu.make_async_remote_copy(
            src_ref=reduced, dst_ref=parts.at[chip], send_sem=part_send, recv_sem=part_recv,
            device_id=(core, lax.rem(me + d, n)), device_id_type=MESH,
        )

    def all_parts(count, semaphore):
        some = parts.at[pl.ds(0, count)]
        pltpu.make_async_copy(some, some, semaphore).wait()

    for d in sorted(range(1, n), key=lambda d: min(d, n - d)):
        part_push(d).start()

    @pl.when(core != g)
    def _():
        part_push(0).start()

    @pl.when(core == g)
    def _():
        parts[chip] = reduced[...]

    merge.wait_send()

    @pl.loop(0, chunks)
    def _(c):
        all_chips(c, tok_send).wait()
        forward(c, core).wait_send()

    loads[4].wait()

    for semaphore in (part_send, part_recv):

        @pl.when(core == g)
        def _():
            all_parts(chips - 1, semaphore)

        @pl.when(core != g)
        def _():
            all_parts(chips, semaphore)

    total = parts[0]
    for p in range(1, chips):
        total = total + parts[p]
    turned = [total] + [pltpu.roll(total, LANES // SEQS * k, axis=1) for k in range(1, SEQS)]

    def tiled(offset):
        out = turned[-offset % SEQS]
        for k in range(1, SEQS):
            out = jnp.where(quarter == k, turned[(k - offset) % SEQS], out)
        return jnp.where(member, out, 0.0)

    left = jnp.concatenate([tiled(0), tiled(1)], axis=0)
    both = jnp.where(lane < rank, turned[2], total)
    right = jnp.concatenate(
        [jnp.where(lane < rank, both, 0.0), jnp.where(lane < rank, 0.0, both)], axis=0
    )
    left_high, left_low = split(left)
    right_high, right_low = split(right)
    kron[...] = lax.dot_general(
        jnp.concatenate([left_high, left_low, left_high], axis=0),
        jnp.concatenate([right_high, right_high, right_low], axis=0),
        (((0,), (0,)), ((), ())),
        preferred_element_type=F32,
    )
    quarters = LANES // SEQS
    kronecker = jnp.concatenate(
        [kron[pl.ds(k, SEQS, stride=quarters), :] for k in range(quarters)], axis=1
    ).astype(BF16)
    scores[...] = dot_lanes(kronecker, qbuf[...])


def ring_call(n, tokens, target, gate, up, down, proj_in, proj_out, segment_ids, queries):
    width, units = gate.shape
    rank = proj_in.shape[1]
    count = segment_ids.shape[0]
    pieces = width // LANES
    any_spec = pl.BlockSpec(memory_space=pl.ANY)
    vmem_spec = pl.BlockSpec(memory_space=pltpu.VMEM)
    dma = pltpu.SemaphoreType.DMA
    return pl.pallas_call(
        functools.partial(ring_kernel, n),
        out_shape=jax.ShapeDtypeStruct((SEQS, queries.shape[0]), F32),
        in_specs=[any_spec] * 7 + [vmem_spec, any_spec],
        out_specs=vmem_spec,
        scratch_shapes=[
            pltpu.VMEM((SLOTS, DEPTH, units), BF16),
            pltpu.VMEM((SLOTS, DEPTH, units), BF16),
            pltpu.VMEM((DOWN_SLOTS, units, DEPTH), BF16),
            pltpu.VMEM((rank, units), BF16),
            pltpu.VMEM((rank, width), BF16),
            pltpu.VMEM((1, width), BF16),
            pltpu.VMEM((1, width), BF16),
            pltpu.VMEM(queries.shape, BF16),
            pltpu.VMEM((pieces, LANES), F32),
            pltpu.VMEM((pieces, LANES), BF16),
            pltpu.VMEM((n, pieces, LANES), BF16),
            pltpu.VMEM((n * pieces, LANES), F32),
            pltpu.VMEM((count, width), BF16),
            pltpu.VMEM((rank, rank * rank), BF16),
            pltpu.VMEM((count, rank * rank), F32),
            pltpu.VMEM((count, units), F32),
            pltpu.VMEM((count, units), F32),
            pltpu.VMEM((count, units), BF16),
            pltpu.VMEM((2 * count, DEPTH), BF16),
            pltpu.VMEM((2 * count, rank), F32),
            pltpu.VMEM((count // 2, 2 * rank), F32),
            pltpu.VMEM((count // 2, 2 * rank), F32),
            pltpu.VMEM((n, count // 2, 2 * rank), F32),
            pltpu.VMEM((n, count // 2, 2 * rank), F32),
            dma((SLOTS,)),
            dma((SLOTS,)),
            dma((DOWN_SLOTS,)),
            dma((5,)),
            dma((n,)),
            dma((n,)),
            dma((n,)),
            dma((n,)),
            dma((n,)),
            dma((n,)),
        ],
        compiler_params=pltpu.CompilerParams(
            collective_id=1, has_side_effects=True, vmem_limit_bytes=63 * 1024 * 1024
        ),
        name="forget_ring",
    )(
        tokens, target, gate, up, down, proj_in.T, proj_out.T,
        segment_ids.reshape(1, count), queries,
    ).T


def pair_call(n, tokens, target, gate, up, down, proj_in, proj_out, segment_ids, queries):
    width, units = gate.shape
    half = units // 2
    rank = proj_in.shape[1]
    pieces = width // LANES
    rows = pieces // CHUNKS
    any_spec = pl.BlockSpec(memory_space=pl.ANY)
    vmem_spec = pl.BlockSpec(memory_space=pltpu.VMEM)
    dma = pltpu.SemaphoreType.DMA
    return pl.pallas_call(
        functools.partial(pair_kernel, n),
        out_shape=jax.ShapeDtypeStruct((SEQS, queries.shape[0]), F32),
        in_specs=[any_spec] * 9,
        out_specs=vmem_spec,
        scratch_shapes=[
            pltpu.VMEM((width, units), BF16),
            pltpu.VMEM((half + ROWS, width), BF16),
            pltpu.VMEM((rank, half), BF16),
            pltpu.VMEM((rank, width), BF16),
            pltpu.VMEM((1, width), BF16),
            pltpu.VMEM((1, width), BF16),
            pltpu.VMEM(queries.shape, BF16),
            pltpu.VMEM((pieces, LANES), F32),
            pltpu.VMEM((pieces, LANES), BF16),
            pltpu.VMEM((CHUNKS, 2 * n, rows, LANES), BF16),
            pltpu.VMEM((max(2 * n * rows, half // LANES * rank), LANES), F32),
            pltpu.VMEM((2 * n, width // CHUNKS), BF16),
            pltpu.SMEM((n,), jnp.int32),
            pltpu.VMEM((2 * n, units), F32),
            pltpu.VMEM((rank, half + ROWS), F32),
            pltpu.VMEM((4 * rank, half + ROWS), BF16),
            pltpu.VMEM((2, n, LANES), F32),
            pltpu.VMEM((n, LANES), F32),
            pltpu.VMEM((n, LANES), F32),
            pltpu.VMEM((n, n, LANES), F32),
            pltpu.VMEM((LANES, LANES), F32),
            dma((FINE,)),
            dma((FINE,)),
            dma((FINE,)),
            dma((6,)),
            dma((CHUNKS,)),
            dma((CHUNKS,)),
            dma((CHUNKS,)),
            dma((CHUNKS,)),
            dma,
            dma,
            dma,
            dma,
        ],
        compiler_params=pltpu.CompilerParams(
            collective_id=0, has_side_effects=True, vmem_limit_bytes=63 * 1024 * 1024
        ),
        name="forget_pair",
    )(tokens, target, gate, up, down, proj_in.T, proj_out.T, segment_ids, queries).T


def solution(mesh):
    n = mesh.shape["query"]
    groups = mesh.shape["groups"]

    def local(tokens, target, gate, up, down, proj_in, proj_out, segment_ids, queries):
        width, units = gate.shape
        shared = (
            groups == 2
            and n == 16
            and segment_ids.shape[0] == n
            and tokens.shape[0] == 1
            and units % (2 * LANES) == 0
            and width % (FINE * LANES) == 0
            and 2 * proj_in.shape[1] == LANES
        )
        call = pair_call if shared else ring_call
        return call(n, tokens, target, gate, up, down, proj_in, proj_out, segment_ids, queries)

    in_specs = (
        P(("groups", "query"), None),
        P(("groups", "query"), None),
        P(None, "query"),
        P(None, "query"),
        P("query", None),
        P("query", None),
        P(),
        P("groups"),
        P("query", None),
    )
    return jax.shard_map(
        local, mesh=mesh, in_specs=in_specs, out_specs=P("query", "groups"), check_vma=False
    )
```
